32 devices in a mesh: seq: 8 (over z, x), head: 4 (over y, core).
Axes of the slice: x: 2, y: 2, z: 4, core: 2. Of those that a mesh axis runs over, the one named last changes fastest.
Arguments:
- queries: bfloat16 [1024, 1024], P('seq', 'head'), may hold values from -6 to 6
- keys: bfloat16 [1024, 1024], P('seq', 'head'), may hold values from -6 to 6
- values: bfloat16 [1024, 1024], P('seq', 'head'), may hold values from -3 to 3
- out_grad: bfloat16 [1024, 1024], P('seq', 'head'), may hold values from -3 to 3
- w_query: bfloat16 [1024, 2048], P('head'), may hold values from -0.1875 to 0.1875
- w_key: bfloat16 [1024, 2048], P('head'), may hold values from -0.1875 to 0.1875
- w_value: bfloat16 [1024, 2048], P('head'), may hold values from -0.1875 to 0.1875
Outputs:
- input_grad: bfloat16 [1024, 2048], P('seq', 'head')
The draws below stay inside these ranges and needn't reach their ends.
All inputs are finite; a program needn't handle non-finite values.
Results may differ from the reference program's by a relative error of at most 0.0064.
Values sent between devices are 32-bit elements; how exact they have to be, the bound alone decides.
A program may use at most 128 MiB of HBM per device.

```python
import jax
import jax.numpy as jnp
import numpy as np
from jax import lax

HD = 64
HEADS = 16
D = 2048
FEATS = 2080
TOK_DEV = 128
TOKENS = 1024
N_SEQ = 8


def block_scale(own_key, dims, shards, low, top_value):
    def one(dim, parts):
        heights = jax.random.uniform(jax.random.fold_in(jax.random.fold_in(own_key, 6), dim), (parts,), jnp.float32, low / len(shards), top_value / len(shards))
        return jnp.repeat(jnp.exp(heights), dims[dim] // parts).reshape((-1,) + (1,) * (len(dims) - dim - 1))

    loudness = one(*shards[0])
    for cut in shards[1:]:
        loudness = loudness * one(*cut)
    return loudness


def gaussian(own_key, extent, spread, reach, shards=(), kind=jnp.bfloat16):
    values = spread * jax.random.normal(own_key, extent, jnp.float32)
    if shards:
        values = values * block_scale(own_key, extent, shards, -0.22, 0.18)
    return jnp.clip(values, -reach, reach).astype(kind)


def setup_inputs(seed: int = 0) -> dict:
    seeds = jax.random.split(jax.random.key(seed), 8)
    queries = gaussian(seeds[0], (TOKENS, HEADS * HD), 1.0, 6.0, ((0, 8), (1, 4)))
    keys = gaussian(seeds[1], (TOKENS, HEADS * HD), 1.0, 6.0, ((0, 8), (1, 4)))
    values = gaussian(seeds[2], (TOKENS, HEADS * HD), 0.5, 3.0, ((0, 8), (1, 4)))
    out_grad = gaussian(seeds[3], (TOKENS, HEADS * HD), 0.5, 3.0, ((0, 8), (1, 4)))
    w_query = gaussian(seeds[4], (HEADS * HD, D), (HEADS * HD) ** -0.5, 0.1875, ((0, 4),))
    w_key = gaussian(seeds[5], (HEADS * HD, D), (HEADS * HD) ** -0.5, 0.1875, ((0, 4),))
    w_value = gaussian(seeds[6], (HEADS * HD, D), (HEADS * HD) ** -0.5, 0.1875, ((0, 4),))
    return {"queries": queries, "keys": keys, "values": values, "out_grad": out_grad, "w_query": w_query, "w_key": w_key, "w_value": w_value}


def pair_tables(width):
    first, second = np.triu_indices(width)
    count = first.shape[0]
    select_first = np.zeros((width, count), np.float32)
    select_second = np.zeros((width, count), np.float32)
    select_first[first, np.arange(count)] = 1.0
    select_second[second, np.arange(count)] = 1.0
    scaling = np.where(first == second, 1.0, np.sqrt(2.0)) / width
    return (select_first, select_second, scaling.astype(np.float32))

def expand_features(inputs, pick_first, pick_second, scaling):
    first = jnp.dot(inputs, pick_first, preferred_element_type=jnp.float32)
    second = jnp.dot(inputs, pick_second, preferred_element_type=jnp.float32)
    return (first.astype(jnp.bfloat16), second.astype(jnp.bfloat16), (first * second * scaling).astype(jnp.bfloat16))

def chain_back(first, second, dphi, back_first, back_second, scaling):
    left = dphi * scaling * second.astype(jnp.float32)
    right = dphi * scaling * first.astype(jnp.float32)
    return jnp.dot(left, back_first, precision=lax.Precision.HIGHEST, preferred_element_type=jnp.float32) + jnp.dot(right, back_second, precision=lax.Precision.HIGHEST, preferred_element_type=jnp.float32)

def reference(queries, keys, values, out_grad, w_query, w_key, w_value):
    select_first, select_second, scale_np = pair_tables(HD)
    pick_first = jnp.asarray(select_first, jnp.bfloat16)
    pick_second = jnp.asarray(select_second, jnp.bfloat16)
    back_first = jnp.asarray(select_first.T, jnp.float32)
    back_second = jnp.asarray(select_second.T, jnp.float32)
    scaling = jnp.asarray(scale_np, jnp.float32)

    def shaped(array):
        return array.reshape(N_SEQ, TOK_DEV, HEADS, HD)
    blocks = (shaped(queries), shaped(keys), shaped(values), shaped(out_grad))
    zero_state = jnp.zeros((FEATS, HEADS, HD), jnp.float32)

    def features_of(array):
        first, second, feats = expand_features(array.reshape(TOK_DEV * HEADS, HD), pick_first, pick_second, scaling)
        return (first, second, feats)

    def state_of(feats, other):
        return jnp.einsum('thf,thd->fhd', feats.reshape(TOK_DEV, HEADS, FEATS).astype(jnp.float32), other.astype(jnp.float32))

    def total_step(total, block):
        query_b, key_b, value_b, grad_b = block
        feats = features_of(query_b)[2]
        return (total + state_of(feats, grad_b), None)
    grad_total, unused = lax.scan(total_step, zero_state, blocks)
    causal = lax.broadcasted_iota(jnp.int32, (TOK_DEV, TOK_DEV), 0) >= lax.broadcasted_iota(jnp.int32, (TOK_DEV, TOK_DEV), 1)

    def step(carry, block):
        kv_sum, grad_sum = carry
        query_b, key_b, value_b, grad_b = block
        qfirst, qsecond, fq = features_of(query_b)
        kfirst, ksecond, fk = features_of(key_b)
        kv_local = state_of(fk, value_b)
        grad_local = state_of(fq, grad_b)
        kv_before = kv_sum.astype(jnp.bfloat16).astype(jnp.float32)
        grad_after = (grad_total - grad_sum - grad_local).astype(jnp.bfloat16).astype(jnp.float32)
        qf = query_b.astype(jnp.float32)
        kf = key_b.astype(jnp.float32)
        vf = value_b.astype(jnp.float32)
        gf = grad_b.astype(jnp.float32)
        scores = jnp.einsum('thd,shd->hts', qf, kf)
        products = jnp.einsum('thd,shd->hts', gf, vf)
        attn = jnp.where(causal, (scores / HD) ** 2, 0.0).astype(jnp.bfloat16).astype(jnp.float32)
        pgrad = jnp.where(causal, 2.0 * scores * products / (HD * HD), 0.0).astype(jnp.bfloat16).astype(jnp.float32)
        dfq = jnp.einsum('thd,fhd->thf', gf, kv_before).reshape(TOK_DEV * HEADS, FEATS)
        dfk = jnp.einsum('thd,fhd->thf', vf, grad_after).reshape(TOK_DEV * HEADS, FEATS)
        query_grad = jnp.einsum('hts,shd->thd', pgrad, kf) + chain_back(qfirst, qsecond, dfq, back_first, back_second, scaling).reshape(TOK_DEV, HEADS, HD)
        key_grad = jnp.einsum('hts,thd->shd', pgrad, qf) + chain_back(kfirst, ksecond, dfk, back_first, back_second, scaling).reshape(TOK_DEV, HEADS, HD)
        value_grad = jnp.einsum('hts,thd->shd', attn, gf) + jnp.einsum('thf,fhd->thd', fk.reshape(TOK_DEV, HEADS, FEATS).astype(jnp.float32), grad_after)
        mixed = jnp.dot(query_grad.astype(jnp.bfloat16).reshape(TOK_DEV, HEADS * HD), w_query, preferred_element_type=jnp.float32)
        mixed = mixed + jnp.dot(key_grad.astype(jnp.bfloat16).reshape(TOK_DEV, HEADS * HD), w_key, preferred_element_type=jnp.float32)
        mixed = mixed + jnp.dot(value_grad.astype(jnp.bfloat16).reshape(TOK_DEV, HEADS * HD), w_value, preferred_element_type=jnp.float32)
        return ((kv_sum + kv_local, grad_sum + grad_local), mixed.astype(jnp.bfloat16))
    unused_carry, result = lax.scan(step, (zero_state, zero_state), blocks)
    return result.reshape(N_SEQ * TOK_DEV, D)
```

```python
import functools

import jax
import jax.numpy as jnp
import numpy as np
from jax import lax
from jax.experimental import pallas as pl
from jax.experimental.pallas import tpu as pltpu
from jax.sharding import PartitionSpec as P

HD = 64
MESH = pl.DeviceIdType.MESH


def shifted(value, axis, steps):
    count = lax.axis_size(axis)
    leading, last = (max(0, -steps), min(count, count - steps))
    return lax.ppermute(value, axis, [(source, source + steps) for source in range(leading, last)])


def pair_tables(width):
    first, second = np.triu_indices(width)
    count = first.shape[0]
    select_first = np.zeros((width, count), np.float32)
    select_second = np.zeros((width, count), np.float32)
    select_first[first, np.arange(count)] = 1.0
    select_second[second, np.arange(count)] = 1.0
    scaling = np.where(first == second, 1.0, np.sqrt(2.0)) / width
    return (select_first, select_second, scaling.astype(np.float32))


def expand_features(inputs, pick_first, pick_second, scaling):
    first = jnp.dot(inputs, pick_first, preferred_element_type=jnp.bfloat16)
    second = jnp.dot(inputs, pick_second, preferred_element_type=jnp.bfloat16)
    feats = (first.astype(jnp.float32) * second.astype(jnp.float32) * scaling).astype(jnp.bfloat16)
    return (first, second, feats)


def chain_back(first, second, dphi, back_first, back_second, scaling):
    scaled = dphi * scaling
    left = scaled * second.astype(jnp.float32)
    right = scaled * first.astype(jnp.float32)
    return jnp.dot(
        left, back_first, precision=lax.Precision.HIGHEST, preferred_element_type=jnp.float32
    ) + jnp.dot(
        right, back_second, precision=lax.Precision.HIGHEST, preferred_element_type=jnp.float32
    )


def on_device(queries, keys, values, out_grad, w_query, w_key, w_value):
    count_rows = queries.shape[0]
    head_count = queries.shape[1] // HD
    select_first, select_second, scale_np = pair_tables(HD)
    pick_first = jnp.asarray(select_first, jnp.bfloat16)
    pick_second = jnp.asarray(select_second, jnp.bfloat16)
    back_first = jnp.asarray(select_first.T, jnp.float32)
    back_second = jnp.asarray(select_second.T, jnp.float32)
    scaling = jnp.asarray(scale_np, jnp.float32)
    feat_count = scale_np.shape[0]
    query_heads = queries.reshape(count_rows, head_count, HD)
    key_heads = keys.reshape(count_rows, head_count, HD)
    value_heads = values.reshape(count_rows, head_count, HD)
    grad_heads = out_grad.reshape(count_rows, head_count, HD)
    query_expanded = []
    key_expanded = []
    kv_parts = []
    grad_parts = []
    for number in range(head_count):
        query_set = expand_features(query_heads[:, number], pick_first, pick_second, scaling)
        key_set = expand_features(key_heads[:, number], pick_first, pick_second, scaling)
        query_expanded.append(query_set)
        key_expanded.append(key_set)
        kv_parts.append(
            jnp.einsum(
                "tf,td->fd", key_set[2], value_heads[:, number], preferred_element_type=jnp.float32
            )
        )
        grad_parts.append(
            jnp.einsum(
                "tf,td->fd", query_set[2], grad_heads[:, number], preferred_element_type=jnp.float32
            )
        )
    kv_local = jnp.stack(kv_parts, 1).reshape(feat_count, head_count * HD)
    grad_local = jnp.stack(grad_parts, 1).reshape(feat_count, head_count * HD)
    rounds = (lax.axis_size("seq") - 1).bit_length()
    kv_running = kv_local
    grad_running = grad_local
    for level in range(rounds):
        kv_running = kv_running + shifted(kv_running, "seq", 1 << level)
        grad_running = grad_running + shifted(grad_running, "seq", -(1 << level))
    kv_before = kv_running - kv_local
    grad_after = grad_running - grad_local
    kv_before = kv_before.astype(jnp.bfloat16).reshape(feat_count, head_count, HD)
    grad_after = grad_after.astype(jnp.bfloat16).reshape(feat_count, head_count, HD)
    causal = lax.broadcasted_iota(jnp.int32, (count_rows, count_rows), 0) >= lax.broadcasted_iota(
        jnp.int32, (count_rows, count_rows), 1
    )
    scores = jnp.einsum("thd,shd->hts", query_heads, key_heads, preferred_element_type=jnp.float32)
    products = jnp.einsum(
        "thd,shd->hts", grad_heads, value_heads, preferred_element_type=jnp.float32
    )
    attn = jnp.where(causal, (scores / HD) ** 2, 0.0).astype(jnp.bfloat16)
    pgrad = jnp.where(causal, 2.0 * scores * products / (HD * HD), 0.0).astype(jnp.bfloat16)
    query_local = jnp.einsum("hts,shd->thd", pgrad, key_heads, preferred_element_type=jnp.float32)
    key_local = jnp.einsum("hts,thd->shd", pgrad, query_heads, preferred_element_type=jnp.float32)
    value_local = jnp.einsum("hts,thd->shd", attn, grad_heads, preferred_element_type=jnp.float32)
    query_out = []
    key_out = []
    value_out = []
    for number in range(head_count):
        qfirst, qsecond, query_feat = query_expanded[number]
        kfirst, ksecond, key_feat = key_expanded[number]
        dfq = jnp.einsum(
            "td,fd->tf",
            grad_heads[:, number],
            kv_before[:, number],
            preferred_element_type=jnp.float32,
        )
        dfk = jnp.einsum(
            "td,fd->tf",
            value_heads[:, number],
            grad_after[:, number],
            preferred_element_type=jnp.float32,
        )
        query_out.append(
            query_local[:, number]
            + chain_back(qfirst, qsecond, dfq, back_first, back_second, scaling)
        )
        key_out.append(
            key_local[:, number]
            + chain_back(kfirst, ksecond, dfk, back_first, back_second, scaling)
        )
        value_out.append(
            value_local[:, number]
            + jnp.einsum(
                "tf,fd->td", key_feat, grad_after[:, number], preferred_element_type=jnp.float32
            )
        )
    query_grad = jnp.stack(query_out, 1).astype(jnp.bfloat16).reshape(count_rows, head_count * HD)
    key_grad = jnp.stack(key_out, 1).astype(jnp.bfloat16).reshape(count_rows, head_count * HD)
    value_grad = jnp.stack(value_out, 1).astype(jnp.bfloat16).reshape(count_rows, head_count * HD)
    partial_sum = jnp.dot(query_grad, w_query, preferred_element_type=jnp.float32)
    partial_sum = partial_sum + jnp.dot(key_grad, w_key, preferred_element_type=jnp.float32)
    partial_sum = partial_sum + jnp.dot(value_grad, w_value, preferred_element_type=jnp.float32)
    return lax.psum_scatter(partial_sum, "head", scatter_dimension=1, tiled=True).astype(
        jnp.bfloat16
    )


def masked(block):
    lanes = lax.broadcasted_iota(jnp.int32, block.shape, 1)
    low = jnp.where(lanes < HD, block, 0.0).astype(jnp.bfloat16)
    high = jnp.where(lanes >= HD, block, 0.0).astype(jnp.bfloat16)
    return low, high


def stacked(block):
    return jnp.concatenate(masked(block), axis=0)


def rows_dot(left, right):
    return lax.dot_general(
        left, right, (((1,), (1,)), ((), ())), preferred_element_type=jnp.float32
    )


def dot(left, right):
    return jnp.dot(left, right, preferred_element_type=jnp.float32)


def pgrad_of(scores, products):
    return scores * products * (2.0 / (HD * HD))


def attn_of(scores):
    scaled = scores * (1.0 / HD)
    return scaled * scaled


K, V, Q, G = range(4)
DQ, DK, DV = range(3)
LINES = 4


def routed_kernel(
    parts,
    k_hbm,
    v_hbm,
    q_hbm,
    g_hbm,
    wq_hbm,
    wk_hbm,
    wv_hbm,
    out,
    own,
    mine,
    inbox,
    side_in,
    plain_r,
    stk_r,
    plain_m,
    stk_m,
    stage_m,
    stage_r,
    stage_a,
    ret,
    weights,
    totals,
    own_part,
    core_send_buf,
    core_recv_buf,
    far_send_buf,
    far_recv_buf,
    own_sem,
    weight_sem,
    mover_send,
    far_send,
    near_send,
    side_send,
    in_recv,
    side_recv,
    ret_recv,
    ret_send_m,
    ret_send_r,
    ret_send_a,
    reduce_send_sem,
    reduce_recv_sem,
):
    unused, rows, width = own.shape
    pairs = width // (2 * HD)
    lane = 2 * HD
    rp = rows // parts
    me = lax.axis_index("seq")
    line, side = me // 2, me % 2
    other = 2 * line + (1 - side)
    head = lax.axis_index("head")
    far, core = head // 2, head % 2
    core_mate = 2 * far + (1 - core)
    far_mate = 2 * (1 - far) + core
    out_width = out.shape[1]
    first_core = core == 0

    site = 1 + core
    is_main = line == site
    base_m = jnp.where(first_core, 4, 0)
    base_r = 4 - base_m
    is_mover = jnp.where(first_core, line >= 2, line < 2)
    is_far = line == 3 * core
    is_near = line == jnp.where(first_core, 3, 1)
    near_line = jnp.where(first_core, 2, 0)
    is_near_site = line == near_line
    has_pair = is_main | is_near_site
    t_line = 2 * (line // 2) + 1
    s_line = t_line - 1
    mover_a = jnp.where(first_core, Q, K)
    resident_c = Q - mover_a

    own_copies = [
        pltpu.make_async_copy(source, own.at[i], own_sem.at[i])
        for i, source in enumerate((k_hbm, v_hbm, q_hbm, g_hbm))
    ]
    for copy in own_copies:
        copy.start()

    barrier = pltpu.get_barrier_semaphore()

    def greet(target):
        pl.semaphore_signal(barrier, inc=1, device_id=target, device_id_type=MESH)

    for step in range(1, 2 * LINES):
        greet({"seq": lax.rem(me + step, 2 * LINES)})
    greet({"head": core_mate})
    greet({"head": far_mate})

    weight_copies = [
        pltpu.make_async_copy(source, weights.at[i], weight_sem.at[i])
        for i, source in enumerate((wq_hbm, wk_hbm, wv_hbm))
    ]
    for copy in weight_copies:
        copy.start()
    for which, copy in enumerate(own_copies):
        copy.wait()
        for p in range(pairs):
            mine[which, p] = own[which, :, lane * p : lane * (p + 1)].astype(jnp.float32)
        inbox[which, me] = mine[which, side]

    pl.semaphore_wait(barrier, 2 * LINES + 1)

    def remote(source, target_ref, send, recv, target):
        return pltpu.make_async_remote_copy(
            src_ref=source,
            dst_ref=target_ref,
            send_sem=send,
            recv_sem=recv,
            device_id={"seq": target},
            device_id_type=MESH,
        )

    def part(r):
        return pl.ds(r * rp, rp)

    def mover_copy(i, p, r):
        w = mover_a + i
        return remote(
            mine.at[w, p, part(r)],
            inbox.at[w, me, part(r)],
            mover_send.at[i, p, r],
            in_recv.at[w, me, r],
            2 * site + p,
        )

    def far_copy(i, p):
        w = resident_c + i
        return remote(
            mine.at[w, p], inbox.at[w, me], far_send.at[i, p], in_recv.at[w, me, 0], 2 * site + p
        )

    def near_copy(i, p):
        w = Q + i
        return remote(
            mine.at[w, p],
            inbox.at[w, me],
            near_send.at[i, p],
            in_recv.at[w, me, 0],
            2 * near_line + p,
        )

    lead = 2 * side

    def lead_copy(i):
        w = lead + i
        return remote(
            mine.at[w, 1 - side], inbox.at[w, me], side_send.at[i], in_recv.at[w, me, 0], other
        )

    def rest_copy(i):
        return remote(
            mine.at[lead + i, side], side_in.at[i], side_send.at[2 + i], side_recv.at[i], other
        )

    def back_copy(i):
        w = 2 - lead + i
        return remote(
            mine.at[w, 1 - side], inbox.at[w, me], side_send.at[4 + i], in_recv.at[w, me, 0], other
        )

    sends_back = jnp.where(side == 1, has_pair, is_main)

    pending = []

    def launch(cond, copies):
        pending.append((cond, copies))
        if cond is None:
            for copy in copies:
                copy.start()
        else:

            @pl.when(cond)
            def _():
                for copy in copies:
                    copy.start()

    launch(is_mover, [mover_copy(i, p, 0) for p in range(pairs) for i in range(2)])
    launch(is_far, [far_copy(i, p) for p in range(pairs) for i in range(2)])
    launch(None, [lead_copy(0), lead_copy(1)])
    launch(sends_back, [back_copy(0), back_copy(1)])
    for r in range(1, parts):
        launch(is_mover, [mover_copy(i, p, r) for p in range(pairs) for i in range(2)])
    launch(None, [rest_copy(0), rest_copy(1)])
    launch(is_near, [near_copy(i, p) for p in range(pairs) for i in range(2)])

    def arrive(w, b, r=None):
        ref = inbox.at[w, b] if r is None else inbox.at[w, b, part(r)]
        sem = in_recv.at[w, b, 0 if r is None else r]
        remote(ref, ref, side_send.at[0], sem, other).wait_recv()

    def columns(p):
        return pl.ds(pl.multiple_of(p * lane, lane), lane)

    def query_role(p, k_block, v_block, diagonal=False):
        k2, v2 = stacked(k_block), stacked(v_block)
        cols = columns(p)
        weight = pgrad_of(rows_dot(own[Q, :, cols], k2), rows_dot(own[G, :, cols], v2))
        if diagonal:
            t = lax.broadcasted_iota(jnp.int32, weight.shape, 0)
            s = lax.broadcasted_iota(jnp.int32, weight.shape, 1) % rows
            weight = jnp.where(t >= s, weight, 0.0)
        result = dot(weight.astype(jnp.bfloat16), k2)
        if diagonal:
            totals[DQ, :, cols] = result
        else:
            totals[DQ, :, cols] += result

    def key_role(p, q_block, g_block, diagonal=False):
        q2, g2 = stacked(q_block), stacked(g_block)
        cols = columns(p)
        scores = rows_dot(own[K, :, cols], q2)
        weight = pgrad_of(scores, rows_dot(own[V, :, cols], g2))
        attn = attn_of(scores)
        if diagonal:
            s = lax.broadcasted_iota(jnp.int32, weight.shape, 0)
            t = lax.broadcasted_iota(jnp.int32, weight.shape, 1) % rows
            weight = jnp.where(t >= s, weight, 0.0)
            attn = jnp.where(t >= s, attn, 0.0)
        key_result = dot(weight.astype(jnp.bfloat16), q2)
        value_result = dot(attn.astype(jnp.bfloat16), g2)
        if diagonal:
            totals[DK, :, cols] = key_result
            totals[DV, :, cols] = value_result
        else:
            totals[DK, :, cols] += key_result
            totals[DV, :, cols] += value_result

    for p in range(pairs):
        query_role(p, mine[K, p], mine[V, p], True)
        key_role(p, mine[Q, p], mine[G, p], True)

    for i in range(2):
        arrive(2 - lead + i, other)
    for i in range(2):
        rest_copy(i).wait_recv()

    @pl.when(side == 1)
    def _():
        query_role(1, inbox[K, other], inbox[V, other])
        query_role(0, side_in[0], side_in[1])

    @pl.when(side == 0)
    def _():
        key_role(0, inbox[Q, other], inbox[G, other])
        key_role(1, side_in[0], side_in[1])

    def give(kind, slot, source, r, send, target):
        return remote(
            source, ret.at[kind, slot, side, part(r)], send, ret_recv.at[kind, slot, side, r], target
        )

    here = columns(side)

    @pl.when(jnp.where(side == 0, has_pair, is_main))
    def _():
        for i in range(2):
            arrive(lead + i, other)

    @pl.when(is_main)
    def _():
        far_base = base_r + 2 * core
        for j in range(2):
            for i in range(2):
                arrive(resident_c + i, far_base + j)

    @pl.when(is_near_site)
    def _():
        for j in range(2):
            for i in range(2):
                arrive(Q + i, 2 * t_line + j)

    def pair_part(w, at_line, j):
        return inbox[w, 2 * at_line + j]

    @pl.when(has_pair)
    def _():
        k_blocks = [pair_part(K, s_line, j) for j in range(2)]
        v_blocks = [pair_part(V, s_line, j) for j in range(2)]
        k2 = jnp.concatenate([stacked(b) for b in k_blocks], axis=0)
        v2 = jnp.concatenate([stacked(b) for b in v_blocks], axis=0)
        for j in range(2):
            q = pair_part(Q, t_line, j).astype(jnp.bfloat16)
            g = pair_part(G, t_line, j).astype(jnp.bfloat16)
            weight = pgrad_of(rows_dot(q, k2), rows_dot(g, v2))
            stage_a[DQ, j] = dot(weight.astype(jnp.bfloat16), k2)
        q2 = jnp.concatenate([stacked(pair_part(Q, t_line, j)) for j in range(2)], axis=0)
        g2 = jnp.concatenate([stacked(pair_part(G, t_line, j)) for j in range(2)], axis=0)
        for j in range(2):
            scores = rows_dot(k_blocks[j].astype(jnp.bfloat16), q2)
            products = rows_dot(v_blocks[j].astype(jnp.bfloat16), g2)
            stage_a[DK, j] = dot(pgrad_of(scores, products).astype(jnp.bfloat16), q2)
            stage_a[DV, j] = dot(attn_of(scores).astype(jnp.bfloat16), g2)

    def pair_give(kind, j, r, slot, target):
        return give(kind, slot, stage_a.at[kind, j, part(r)], r, ret_send_a.at[kind, j, r], target)

    t_here = t_line == line
    s_here = jnp.logical_not(t_here)
    lower_near = jnp.where(first_core, 0, 1)
    s_slot = jnp.where(is_near_site, lower_near, 0)
    t_slot = jnp.where(is_near_site, 1 - lower_near, 0)

    every = [(j, r) for r in range(parts) for j in range(2)]
    launch(
        has_pair & t_here,
        [pair_give(DQ, 1 - side, r, 0, other) for r in range(parts)],
    )
    launch(
        has_pair & s_here,
        [pair_give(kind, 1 - side, r, s_slot, other) for r in range(parts) for kind in (DK, DV)],
    )
    @pl.when(has_pair & t_here)
    def _():
        totals[DQ, :, here] += stage_a[DQ, side]

    @pl.when(has_pair & s_here)
    def _():
        for kind in (DK, DV):
            totals[kind, :, here] += stage_a[kind, side]

    launch(is_near_site, [pair_give(DQ, j, r, t_slot, 2 * t_line + j) for j, r in every])

    def mover_give(i, j, r):
        kind = jnp.where(first_core, DQ, DK) + i
        return give(
            kind,
            0,
            stage_m.at[i, r, pl.ds(j * rp, rp)],
            r,
            ret_send_m.at[i, j, r],
            base_m + j,
        )

    def resident_give(i, j, r):
        kind = jnp.where(first_core, DK, DQ) + i
        return give(
            kind, 0, stage_r.at[i, j, part(r)], r, ret_send_r.at[i, j, r], base_r + j
        )

    far_j = 2 * core
    near_j = 2 * (1 - core)

    @pl.when(is_main)
    def _():
        for j in range(4):
            for i in range(2):
                block = inbox[resident_c + i, base_r + j]
                plain_r[i, j] = block.astype(jnp.bfloat16)
                stk_r[i, j] = stacked(block)
        for i in range(2):
            for j in range(4):
                stage_r[i, j] = jnp.zeros((rows, lane), jnp.float32)

        @pl.when(first_core)
        def _():
            for j in range(2):
                stage_r[0, j] = stage_a[DK, j]
                stage_r[1, j] = stage_a[DV, j]

        @pl.when(core == 1)
        def _():
            for j in range(2):
                stage_r[0, 2 + j] = stage_a[DQ, j]

    for r in range(parts):

        @pl.when(is_main)
        def _(r=r):
            for j in range(4):
                for i in range(2):
                    arrive(mover_a + i, base_m + j, r)
            for j in range(4):
                for i in range(2):
                    block = inbox[mover_a + i, base_m + j, part(r)]
                    low, high = masked(block)
                    at = slice(j * rp, (j + 1) * rp)
                    plain_m[i, r, at] = block.astype(jnp.bfloat16)
                    stk_m[i, r, 0, at] = low
                    stk_m[i, r, 1, at] = high
            flat = 4 * rp
            for first in range(0, flat, rows):
                at = slice(first, first + rows)
                for j in range(4):
                    scores = rows_dot(plain_m[0, r, at], stk_r[0, j])
                    products = rows_dot(plain_m[1, r, at], stk_r[1, j])
                    weight = pgrad_of(scores, products).astype(jnp.bfloat16)
                    result = dot(weight, stk_r[0, j])
                    if j:
                        stage_m[0, r, at] += result
                    else:
                        stage_m[0, r, at] = result

                    @pl.when(core == 1)
                    def _():
                        extra = dot(attn_of(scores).astype(jnp.bfloat16), stk_r[1, j])
                        if j:
                            stage_m[1, r, at] += extra
                        else:
                            stage_m[1, r, at] = extra

        launch(is_main, [mover_give(0, j, r) for j in range(4)])
        launch(is_main & (core == 1), [mover_give(1, j, r) for j in range(4)])

        @pl.when(is_main)
        def _(r=r):
            a2 = stk_m[0, r].reshape(8 * rp, lane)
            b2 = stk_m[1, r].reshape(8 * rp, lane)
            for j in range(4):
                scores = rows_dot(plain_r[0, j], a2)
                products = rows_dot(plain_r[1, j], b2)
                weight = pgrad_of(scores, products).astype(jnp.bfloat16)
                stage_r[0, j] += dot(weight, a2)

                @pl.when(first_core)
                def _():
                    stage_r[1, j] += dot(attn_of(scores).astype(jnp.bfloat16), b2)

    launch(is_main, [resident_give(0, far_j + j, r) for j, r in every])
    launch(is_main & first_core, [resident_give(1, far_j + j, r) for j, r in every])
    launch(is_main, [resident_give(0, near_j + 1 - side, r) for r in range(parts)])
    launch(is_main & first_core, [resident_give(1, near_j + 1 - side, r) for r in range(parts)])

    @pl.when(is_main & first_core)
    def _():
        totals[DK, :, here] += stage_r[0, near_j + side]
        totals[DV, :, here] += stage_r[1, near_j + side]

    @pl.when(is_main & (core == 1))
    def _():
        totals[DQ, :, here] += stage_r[0, near_j + side]

    def taken(kind, slot, p):
        away = side != p
        if kind == DQ:
            if slot == 0:
                return jnp.where(is_main, away, (line == 3) | (line == 3 - site))
            return first_core & (line == 3)
        if slot == 0:
            return (line < 3) & jnp.where(is_main | (line == 2), away, True)
        return (core == 1) & (line == 0) & away

    def take(kind, slot, p, r):
        ref = ret.at[kind, slot, p, part(r)]
        remote(ref, ref, side_send.at[0], ret_recv.at[kind, slot, p, r], other).wait_recv()
        at = slice(r * rp, (r + 1) * rp)
        cols = slice(lane * p, lane * (p + 1))
        totals[kind, at, cols] += ret[kind, slot, p, at]

    def collect(r):
        for slot in (1, 0):
            for kinds in ((DQ,), (DK, DV)):
                for p in range(pairs):

                    @pl.when(taken(kinds[0], slot, p))
                    def _():
                        for kind in kinds:
                            take(kind, slot, p, r)

    def to_head(source, target_ref, n, target):
        return pltpu.make_async_remote_copy(
            src_ref=source,
            dst_ref=target_ref,
            send_sem=reduce_send_sem.at[n],
            recv_sem=reduce_recv_sem.at[n],
            device_id={"head": target},
            device_id_type=MESH,
        )

    def to_core(r, n):
        return to_head(core_send_buf.at[r, n], core_recv_buf.at[r, n], 3 * r + n, core_mate)

    def to_far(r):
        return to_head(far_send_buf.at[r], far_recv_buf.at[r], 3 * r + 2, far_mate)

    for r in range(parts):
        collect(r)
        at = slice(r * rp, (r + 1) * rp)
        if r == 0:
            for copy in weight_copies:
                copy.wait()
        final = [totals[i, at].astype(jnp.bfloat16) for i in range(3)]

        def project(target):
            cols = pl.ds(pl.multiple_of(target * out_width, out_width), out_width)
            return sum(dot(final[i], weights[i, :, cols]) for i in range(3))

        core_send_buf[r, 0] = project(2 * (1 - far) + (1 - core))
        to_core(r, 0).start()
        far_send_buf[r] = project(far_mate)
        to_core(r, 0).wait_recv()
        far_send_buf[r] += core_recv_buf[r, 0]
        to_far(r).start()
        core_send_buf[r, 1] = project(core_mate)
        to_core(r, 1).start()
        own_part[at] = project(head)

    for r in range(parts):
        at = slice(r * rp, (r + 1) * rp)
        to_core(r, 1).wait_recv()
        own_part[at] += core_recv_buf[r, 1]
    for r in range(parts):
        at = slice(r * rp, (r + 1) * rp)
        to_far(r).wait_recv()
        out[at] = (own_part[at] + far_recv_buf[r]).astype(out.dtype)

    for r in range(parts):
        to_core(r, 0).wait_send()
        to_core(r, 1).wait_send()
        to_far(r).wait_send()
    for cond, copies in pending:
        if cond is None:
            for copy in copies:
                copy.wait_send()
        else:

            @pl.when(cond)
            def _(copies=copies):
                for copy in copies:
                    copy.wait_send()


def routed_form(n_head, queries, keys, values, out_grad, w_query, w_key, w_value):
    rows, width = queries.shape
    model = w_query.shape[1]
    out_width = model // n_head
    pairs = width // (2 * HD)
    lane = 2 * HD
    blocks = 2 * LINES
    parts = 2
    rp = rows // parts
    f32, bf16 = jnp.float32, jnp.bfloat16
    dma = pltpu.SemaphoreType.DMA
    return pl.pallas_call(
        functools.partial(routed_kernel, parts),
        out_shape=jax.ShapeDtypeStruct((rows, out_width), bf16),
        in_specs=[pl.BlockSpec(memory_space=pl.ANY)] * 7,
        out_specs=pl.BlockSpec(memory_space=pltpu.VMEM),
        scratch_shapes=[
            pltpu.VMEM((4, rows, width), bf16),
            pltpu.VMEM((4, pairs, rows, lane), f32),
            pltpu.VMEM((4, blocks, rows, lane), f32),
            pltpu.VMEM((2, rows, lane), f32),
            pltpu.VMEM((2, 4, rows, lane), bf16),
            pltpu.VMEM((2, 4, 2 * rows, lane), bf16),
            pltpu.VMEM((2, parts, 4 * rp, lane), bf16),
            pltpu.VMEM((2, parts, 2, 4 * rp, lane), bf16),
            pltpu.VMEM((2, parts, 4 * rp, lane), f32),
            pltpu.VMEM((2, 4, rows, lane), f32),
            pltpu.VMEM((3, 2, rows, lane), f32),
            pltpu.VMEM((3, 2, pairs, rows, lane), f32),
            pltpu.VMEM((3, width, model), bf16),
            pltpu.VMEM((3, rows, width), f32),
            pltpu.VMEM((rows, out_width), f32),
            pltpu.VMEM((parts, 2, rp, out_width), f32),
            pltpu.VMEM((parts, 2, rp, out_width), f32),
            pltpu.VMEM((parts, rp, out_width), f32),
            pltpu.VMEM((parts, rp, out_width), f32),
            dma((4,)),
            dma((3,)),
            dma((2, pairs, parts)),
            dma((2, pairs)),
            dma((2, pairs)),
            dma((6,)),
            dma((4, blocks, parts)),
            dma((2,)),
            dma((3, 2, pairs, parts)),
            dma((2, 4, parts)),
            dma((2, 4, parts)),
            dma((3, 2, parts)),
            dma((3 * parts,)),
            dma((3 * parts,)),
        ],
        compiler_params=pltpu.CompilerParams(collective_id=0, has_side_effects=True),
    )(keys, values, queries, out_grad, w_query, w_key, w_value)


def solution(mesh):
    placed = (
        P("seq", "head"),
        P("seq", "head"),
        P("seq", "head"),
        P("seq", "head"),
        P("head", None),
        P("head", None),
        P("head", None),
    )
    n_seq, n_head = mesh.shape["seq"], mesh.shape["head"]

    def per_device(queries, *rest):
        if n_seq == 2 * LINES and n_head == 4 and queries.shape[1] == 4 * HD:
            return routed_form(n_head, queries, *rest)
        return on_device(queries, *rest)

    return jax.shard_map(
        per_device, mesh=mesh, in_specs=placed, out_specs=P("seq", "head"), check_vma=False
    )
```

```python
import functools

import jax
import jax.numpy as jnp
import numpy as np
from jax import lax
from jax.experimental import pallas as pl
from jax.experimental.pallas import tpu as pltpu
from jax.sharding import PartitionSpec as P

HD = 64
MESH = pl.DeviceIdType.MESH


def shifted(value, axis, steps):
    count = lax.axis_size(axis)
    leading, last = (max(0, -steps), min(count, count - steps))
    return lax.ppermute(value, axis, [(source, source + steps) for source in range(leading, last)])


def pair_tables(width):
    first, second = np.triu_indices(width)
    count = first.shape[0]
    select_first = np.zeros((width, count), np.float32)
    select_second = np.zeros((width, count), np.float32)
    select_first[first, np.arange(count)] = 1.0
    select_second[second, np.arange(count)] = 1.0
    scaling = np.where(first == second, 1.0, np.sqrt(2.0)) / width
    return (select_first, select_second, scaling.astype(np.float32))


def expand_features(inputs, pick_first, pick_second, scaling):
    first = jnp.dot(inputs, pick_first, preferred_element_type=jnp.bfloat16)
    second = jnp.dot(inputs, pick_second, preferred_element_type=jnp.bfloat16)
    feats = (first.astype(jnp.float32) * second.astype(jnp.float32) * scaling).astype(jnp.bfloat16)
    return (first, second, feats)


def chain_back(first, second, dphi, back_first, back_second, scaling):
    scaled = dphi * scaling
    left = scaled * second.astype(jnp.float32)
    right = scaled * first.astype(jnp.float32)
    return jnp.dot(
        left, back_first, precision=lax.Precision.HIGHEST, preferred_element_type=jnp.float32
    ) + jnp.dot(
        right, back_second, precision=lax.Precision.HIGHEST, preferred_element_type=jnp.float32
    )


def on_device(queries, keys, values, out_grad, w_query, w_key, w_value):
    count_rows = queries.shape[0]
    head_count = queries.shape[1] // HD
    select_first, select_second, scale_np = pair_tables(HD)
    pick_first = jnp.asarray(select_first, jnp.bfloat16)
    pick_second = jnp.asarray(select_second, jnp.bfloat16)
    back_first = jnp.asarray(select_first.T, jnp.float32)
    back_second = jnp.asarray(select_second.T, jnp.float32)
    scaling = jnp.asarray(scale_np, jnp.float32)
    feat_count = scale_np.shape[0]
    query_heads = queries.reshape(count_rows, head_count, HD)
    key_heads = keys.reshape(count_rows, head_count, HD)
    value_heads = values.reshape(count_rows, head_count, HD)
    grad_heads = out_grad.reshape(count_rows, head_count, HD)
    query_expanded = []
    key_expanded = []
    kv_parts = []
    grad_parts = []
    for number in range(head_count):
        query_set = expand_features(query_heads[:, number], pick_first, pick_second, scaling)
        key_set = expand_features(key_heads[:, number], pick_first, pick_second, scaling)
        query_expanded.append(query_set)
        key_expanded.append(key_set)
        kv_parts.append(
            jnp.einsum(
                "tf,td->fd", key_set[2], value_heads[:, number], preferred_element_type=jnp.float32
            )
        )
        grad_parts.append(
            jnp.einsum(
                "tf,td->fd", query_set[2], grad_heads[:, number], preferred_element_type=jnp.float32
            )
        )
    kv_local = jnp.stack(kv_parts, 1).reshape(feat_count, head_count * HD)
    grad_local = jnp.stack(grad_parts, 1).reshape(feat_count, head_count * HD)
    rounds = (lax.axis_size("seq") - 1).bit_length()
    kv_running = kv_local
    grad_running = grad_local
    for level in range(rounds):
        kv_running = kv_running + shifted(kv_running, "seq", 1 << level)
        grad_running = grad_running + shifted(grad_running, "seq", -(1 << level))
    kv_before = kv_running - kv_local
    grad_after = grad_running - grad_local
    kv_before = kv_before.astype(jnp.bfloat16).reshape(feat_count, head_count, HD)
    grad_after = grad_after.astype(jnp.bfloat16).reshape(feat_count, head_count, HD)
    causal = lax.broadcasted_iota(jnp.int32, (count_rows, count_rows), 0) >= lax.broadcasted_iota(
        jnp.int32, (count_rows, count_rows), 1
    )
    scores = jnp.einsum("thd,shd->hts", query_heads, key_heads, preferred_element_type=jnp.float32)
    products = jnp.einsum(
        "thd,shd->hts", grad_heads, value_heads, preferred_element_type=jnp.float32
    )
    attn = jnp.where(causal, (scores / HD) ** 2, 0.0).astype(jnp.bfloat16)
    pgrad = jnp.where(causal, 2.0 * scores * products / (HD * HD), 0.0).astype(jnp.bfloat16)
    query_local = jnp.einsum("hts,shd->thd", pgrad, key_heads, preferred_element_type=jnp.float32)
    key_local = jnp.einsum("hts,thd->shd", pgrad, query_heads, preferred_element_type=jnp.float32)
    value_local = jnp.einsum("hts,thd->shd", attn, grad_heads, preferred_element_type=jnp.float32)
    query_out = []
    key_out = []
    value_out = []
    for number in range(head_count):
        qfirst, qsecond, query_feat = query_expanded[number]
        kfirst, ksecond, key_feat = key_expanded[number]
        dfq = jnp.einsum(
            "td,fd->tf",
            grad_heads[:, number],
            kv_before[:, number],
            preferred_element_type=jnp.float32,
        )
        dfk = jnp.einsum(
            "td,fd->tf",
            value_heads[:, number],
            grad_after[:, number],
            preferred_element_type=jnp.float32,
        )
        query_out.append(
            query_local[:, number]
            + chain_back(qfirst, qsecond, dfq, back_first, back_second, scaling)
        )
        key_out.append(
            key_local[:, number]
            + chain_back(kfirst, ksecond, dfk, back_first, back_second, scaling)
        )
        value_out.append(
            value_local[:, number]
            + jnp.einsum(
                "tf,fd->td", key_feat, grad_after[:, number], preferred_element_type=jnp.float32
            )
        )
    query_grad = jnp.stack(query_out, 1).astype(jnp.bfloat16).reshape(count_rows, head_count * HD)
    key_grad = jnp.stack(key_out, 1).astype(jnp.bfloat16).reshape(count_rows, head_count * HD)
    value_grad = jnp.stack(value_out, 1).astype(jnp.bfloat16).reshape(count_rows, head_count * HD)
    partial_sum = jnp.dot(query_grad, w_query, preferred_element_type=jnp.float32)
    partial_sum = partial_sum + jnp.dot(key_grad, w_key, preferred_element_type=jnp.float32)
    partial_sum = partial_sum + jnp.dot(value_grad, w_value, preferred_element_type=jnp.float32)
    return lax.psum_scatter(partial_sum, "head", scatter_dimension=1, tiled=True).astype(
        jnp.bfloat16
    )


def masked(block):
    lanes = lax.broadcasted_iota(jnp.int32, block.shape, 1)
    low = jnp.where(lanes < HD, block, 0.0).astype(jnp.bfloat16)
    high = jnp.where(lanes >= HD, block, 0.0).astype(jnp.bfloat16)
    return low, high


def stacked(block):
    return jnp.concatenate(masked(block), axis=0)


def rows_dot(left, right):
    return lax.dot_general(
        left, right, (((1,), (1,)), ((), ())), preferred_element_type=jnp.float32
    )


def dot(left, right):
    return jnp.dot(left, right, preferred_element_type=jnp.float32)


def pgrad_of(scores, products):
    return scores * products * (2.0 / (HD * HD))


def attn_of(scores):
    scaled = scores * (1.0 / HD)
    return scaled * scaled


K, V, Q, G = range(4)
DQ, DK, DV = range(3)
LINES = 4


def routed_kernel(
    parts,
    k_hbm,
    v_hbm,
    q_hbm,
    g_hbm,
    wq_hbm,
    wk_hbm,
    wv_hbm,
    out,
    own,
    mine,
    inbox,
    side_in,
    plain_r,
    stk_r,
    plain_m,
    stk_m,
    stage_m,
    stage_r,
    stage_a,
    ret,
    weights,
    totals,
    own_part,
    core_send_buf,
    core_recv_buf,
    far_send_buf,
    far_recv_buf,
    own_sem,
    weight_sem,
    mover_send,
    far_send,
    near_send,
    side_send,
    in_recv,
    side_recv,
    ret_recv,
    ret_send_m,
    ret_send_r,
    ret_send_a,
    reduce_send_sem,
    reduce_recv_sem,
):
    unused, rows, width = own.shape
    pairs = width // (2 * HD)
    lane = 2 * HD
    rp = rows // parts
    me = lax.axis_index("seq")
    line, side = me // 2, me % 2
    other = 2 * line + (1 - side)
    head = lax.axis_index("head")
    far, core = head // 2, head % 2
    core_mate = 2 * far + (1 - core)
    far_mate = 2 * (1 - far) + core
    out_width = out.shape[1]
    first_core = core == 0

    site = 1 + core
    is_main = line == site
    base_m = jnp.where(first_core, 4, 0)
    base_r = 4 - base_m
    is_mover = jnp.where(first_core, line >= 2, line < 2)
    is_far = line == 3 * core
    inner = (line == 1) | (line == 2)
    outer = jnp.logical_not(inner)
    near_target = jnp.where(line == 1, 0, 3)
    t_line = jnp.where(line < 2, 1, 3)
    s_line = t_line - 1
    skips = line % 2 != core
    mover_a = jnp.where(first_core, Q, K)
    resident_c = Q - mover_a
    has_up, has_down = line < LINES - 1, line > 0

    own_copies = [
        pltpu.make_async_copy(source, own.at[i], own_sem.at[i])
        for i, source in enumerate((k_hbm, v_hbm, q_hbm, g_hbm))
    ]
    for copy in own_copies:
        copy.start()

    barrier = pltpu.get_barrier_semaphore()

    def greet(target):
        pl.semaphore_signal(barrier, inc=1, device_id=target, device_id_type=MESH)

    greet({"seq": other})
    greet({"head": core_mate})
    greet({"head": far_mate})
    for cond, there in ((has_up, line + 1), (has_down, line - 1), (skips, 4 - 2 * core - line)):

        @pl.when(cond)
        def _(there=there):
            for p in range(2):
                greet({"seq": 2 * there + p})

    weight_copies = [
        pltpu.make_async_copy(source, weights.at[i], weight_sem.at[i])
        for i, source in enumerate((wq_hbm, wk_hbm, wv_hbm))
    ]
    for copy in weight_copies:
        copy.start()
    for which, copy in enumerate(own_copies):
        copy.wait()
        for p in range(pairs):
            mine[which, p] = own[which, :, lane * p : lane * (p + 1)].astype(jnp.float32)
        inbox[which, me] = mine[which, side]

    pl.semaphore_wait(
        barrier,
        3
        + 2
        * (
            has_up.astype(jnp.int32)
            + has_down.astype(jnp.int32)
            + skips.astype(jnp.int32)
        ),
    )

    def remote(source, target_ref, send, recv, target):
        return pltpu.make_async_remote_copy(
            src_ref=source,
            dst_ref=target_ref,
            send_sem=send,
            recv_sem=recv,
            device_id={"seq": target},
            device_id_type=MESH,
        )

    def part(r):
        return pl.ds(r * rp, rp)

    def mover_copy(i, p, r):
        w = mover_a + i
        return remote(
            mine.at[w, p, part(r)],
            inbox.at[w, me, part(r)],
            mover_send.at[i, p, r],
            in_recv.at[w, me, r],
            2 * site + p,
        )

    def whole_copy(w, p, send, target):
        return remote(mine.at[w, p], inbox.at[w, me], send, in_recv.at[w, me, 0], target)

    def far_copy(i, p):
        return whole_copy(resident_c + i, p, far_send.at[i, p], 2 * site + p)

    def near_copy(i, p):
        return whole_copy(near_a + i, p, near_send.at[i, p], 2 * near_target + p)

    lead = 2 * side
    near_a = jnp.where(line % 2 == 1, Q, K)
    needed = jnp.where(outer, 2 * (line // 2), resident_c)
    plain = inner & jnp.logical_not(is_main)
    sent = jnp.where(plain, lead, needed)
    got = jnp.where(plain, 2 - lead, needed)
    leads, led = sent != lead, got != 2 - lead

    def exchange_copy(i):
        return whole_copy(sent + i, 1 - side, side_send.at[i], other)

    def lead_copy(i):
        return whole_copy(lead + i, 1 - side, side_send.at[4 + i], other)

    def rest_copy(i):
        return remote(
            mine.at[lead + i, side], side_in.at[i], side_send.at[2 + i], side_recv.at[i], other
        )

    pending = []

    def launch(cond, copies, again=False):
        if not again:
            pending.append((cond, copies))
        if cond is None:
            for copy in copies:
                copy.start()
        else:

            @pl.when(cond)
            def _():
                for copy in copies:
                    copy.start()

    crossing = [(i, p) for p in range(pairs) for i in range(2)]
    movers_of = [[mover_copy(i, p, r) for i, p in crossing] for r in range(parts)]
    far_copies = [far_copy(i, p) for i, p in crossing]
    near_copies = [near_copy(i, p) for i, p in crossing]
    exchanges = [exchange_copy(i) for i in range(2)]
    lead_copies = [lead_copy(i) for i in range(2)]
    rest_copies = [rest_copy(i) for i in range(2)]

    launch(is_mover, movers_of[0])
    launch(is_far, far_copies)
    launch(jnp.logical_not(plain), exchanges)
    launch(inner, near_copies)

    def arrive(w, b, r=None):
        ref = inbox.at[w, b] if r is None else inbox.at[w, b, part(r)]
        sem = in_recv.at[w, b, 0 if r is None else r]
        remote(ref, ref, side_send.at[0], sem, other).wait_recv()

    def columns(p):
        return pl.ds(pl.multiple_of(p * lane, lane), lane)

    def query_role(p, k_block, v_block, diagonal=False):
        k2, v2 = stacked(k_block), stacked(v_block)
        cols = columns(p)
        weight = pgrad_of(rows_dot(own[Q, :, cols], k2), rows_dot(own[G, :, cols], v2))
        if diagonal:
            t = lax.broadcasted_iota(jnp.int32, weight.shape, 0)
            s = lax.broadcasted_iota(jnp.int32, weight.shape, 1) % rows
            weight = jnp.where(t >= s, weight, 0.0)
        result = dot(weight.astype(jnp.bfloat16), k2)
        if diagonal:
            totals[DQ, :, cols] = result
        else:
            totals[DQ, :, cols] += result

    def key_role(p, q_block, g_block, diagonal=False):
        q2, g2 = stacked(q_block), stacked(g_block)
        cols = columns(p)
        scores = rows_dot(own[K, :, cols], q2)
        weight = pgrad_of(scores, rows_dot(own[V, :, cols], g2))
        attn = attn_of(scores)
        if diagonal:
            s = lax.broadcasted_iota(jnp.int32, weight.shape, 0)
            t = lax.broadcasted_iota(jnp.int32, weight.shape, 1) % rows
            weight = jnp.where(t >= s, weight, 0.0)
            attn = jnp.where(t >= s, attn, 0.0)
        key_result = dot(weight.astype(jnp.bfloat16), q2)
        value_result = dot(attn.astype(jnp.bfloat16), g2)
        if diagonal:
            totals[DK, :, cols] = key_result
            totals[DV, :, cols] = value_result
        else:
            totals[DK, :, cols] += key_result
            totals[DV, :, cols] += value_result

    for p in range(pairs):
        query_role(p, mine[K, p], mine[V, p], True)
        key_role(p, mine[Q, p], mine[G, p], True)

    for r in range(1, parts):
        launch(is_mover, movers_of[r])
    launch(plain, exchanges)
    launch(leads, lead_copies)
    launch(None, rest_copies)
    for i in range(2):
        arrive(got + i, other)

    def give(kind, slot, source, r, send, target):
        return remote(
            source, ret.at[kind, slot, side, part(r)], send, ret_recv.at[kind, slot, side, r], target
        )

    here = columns(side)
    every = [(j, r) for r in range(parts) for j in range(2)]

    def mover_give(i, j, r):
        kind = jnp.where(first_core, DQ, DK) + i
        return give(
            kind,
            0,
            stage_m.at[i, r, pl.ds(j * rp, rp)],
            r,
            ret_send_m.at[i, j, r],
            base_m + j,
        )

    def resident_give(i, j, r):
        kind = jnp.where(first_core, DK, DQ) + i
        return give(
            kind, 0, stage_r.at[i, j, part(r)], r, ret_send_r.at[i, j, r], base_r + j
        )

    far_j = 2 * core
    near_j = 2 * (1 - core)
    flat = 4 * rp

    @pl.when(is_main)
    def _():
        for j in range(2):
            for i in range(2):
                arrive(resident_c + i, base_r + far_j + j)
        for j in range(4):
            for i in range(2):
                block = inbox[resident_c + i, base_r + j]
                plain_r[i, j] = block.astype(jnp.bfloat16)
                stk_r[i, j] = stacked(block)

    def resident_major(both):
        for j in range(4):
            grad_c = grad_d = None
            for r in range(parts):
                a2 = stk_m[0, r].reshape(2 * flat, lane)
                b2 = stk_m[1, r].reshape(2 * flat, lane)
                scores = rows_dot(plain_r[0, j], a2)
                products = rows_dot(plain_r[1, j], b2)
                term = dot(pgrad_of(scores, products).astype(jnp.bfloat16), a2)
                grad_c = term if grad_c is None else grad_c + term
                if both:
                    term = dot(attn_of(scores).astype(jnp.bfloat16), b2)
                    grad_d = term if grad_d is None else grad_d + term
            stage_r[0, j] = grad_c
            if both:
                stage_r[1, j] = grad_d

    for r in range(parts):

        @pl.when(is_main)
        def _(r=r):
            for j in range(4):
                for i in range(2):
                    arrive(mover_a + i, base_m + j, r)
            for j in range(4):
                for i in range(2):
                    block = inbox[mover_a + i, base_m + j, part(r)]
                    low, high = masked(block)
                    at = slice(j * rp, (j + 1) * rp)
                    plain_m[i, r, at] = block.astype(jnp.bfloat16)
                    stk_m[i, r, 0, at] = low
                    stk_m[i, r, 1, at] = high

        def mover_major(both, r=r):
            for first in range(0, flat, rows):
                at = slice(first, first + rows)
                grad_a = grad_b = None
                for j in range(4):
                    scores = rows_dot(plain_m[0, r, at], stk_r[0, j])
                    products = rows_dot(plain_m[1, r, at], stk_r[1, j])
                    term = dot(pgrad_of(scores, products).astype(jnp.bfloat16), stk_r[0, j])
                    grad_a = term if grad_a is None else grad_a + term
                    if both:
                        term = dot(attn_of(scores).astype(jnp.bfloat16), stk_r[1, j])
                        grad_b = term if grad_b is None else grad_b + term
                stage_m[0, r, at] = grad_a
                if both:
                    stage_m[1, r, at] = grad_b

        if r == parts - 1:
            pl.when(is_main & first_core)(lambda: resident_major(True))
            launch(is_main & first_core, [resident_give(i, far_j + j, r) for j, r in every for i in range(2)])
            launch(is_main & first_core, [resident_give(i, near_j + 1 - side, r) for r in range(parts) for i in range(2)])
            for n in range(parts):
                pl.when(is_main & first_core)(lambda: mover_major(False, n))
                launch(is_main & first_core, [mover_give(0, j, n) for j in range(4)])
        pl.when(is_main & (core == 1))(lambda: mover_major(True))
        launch(is_main & (core == 1), [mover_give(i, j, r) for j in range(4) for i in range(2)])

    pl.when(is_main & (core == 1))(lambda: resident_major(False))
    launch(is_main & (core == 1), [resident_give(0, far_j + j, r) for j, r in every])
    launch(is_main & (core == 1), [resident_give(0, near_j + 1 - side, r) for r in range(parts)])

    @pl.when(is_main & first_core)
    def _():
        totals[DK, :, here] += stage_r[0, near_j + side]
        totals[DV, :, here] += stage_r[1, near_j + side]

    @pl.when(is_main & (core == 1))
    def _():
        totals[DQ, :, here] += stage_r[0, near_j + side]

    @pl.when(outer)
    def _():
        from_line = jnp.where(line == 0, 1, 2)
        for j in range(2):
            for i in range(2):
                arrive(Q - needed + i, 2 * from_line + j)

    def pair_part(w, at_line, j):
        return inbox[w, 2 * at_line + j]

    @pl.when(outer)
    def _():
        k_blocks = [pair_part(K, s_line, j) for j in range(2)]
        v_blocks = [pair_part(V, s_line, j) for j in range(2)]
        k2 = jnp.concatenate([stacked(b) for b in k_blocks], axis=0)
        v2 = jnp.concatenate([stacked(b) for b in v_blocks], axis=0)
        for j in range(2):
            q = pair_part(Q, t_line, j).astype(jnp.bfloat16)
            g = pair_part(G, t_line, j).astype(jnp.bfloat16)
            weight = pgrad_of(rows_dot(q, k2), rows_dot(g, v2))
            stage_a[DQ, j] = dot(weight.astype(jnp.bfloat16), k2)
        q2 = jnp.concatenate([stacked(pair_part(Q, t_line, j)) for j in range(2)], axis=0)
        g2 = jnp.concatenate([stacked(pair_part(G, t_line, j)) for j in range(2)], axis=0)
        for j in range(2):
            scores = rows_dot(k_blocks[j].astype(jnp.bfloat16), q2)
            products = rows_dot(v_blocks[j].astype(jnp.bfloat16), g2)
            stage_a[DK, j] = dot(pgrad_of(scores, products).astype(jnp.bfloat16), q2)
            stage_a[DV, j] = dot(attn_of(scores).astype(jnp.bfloat16), g2)

    def pair_give(kind, j, r, target):
        slot = jnp.where(target == other, 1, 0)
        return give(kind, slot, stage_a.at[kind, j, part(r)], r, ret_send_a.at[kind, j, r], target)

    def pair_gives(kinds, j, target):
        return [pair_give(kind, j, r, target) for r in range(parts) for kind in kinds]

    t_here, s_here = line == 3, line == 0
    launch(s_here, [c for j in range(2) for c in pair_gives((DQ,), j, 2 * t_line + j)])
    launch(s_here, pair_gives((DK, DV), 1 - side, other))
    launch(t_here, [c for j in range(2) for c in pair_gives((DK, DV), j, 2 * s_line + j)])
    launch(t_here, pair_gives((DQ,), 1 - side, other))

    @pl.when(t_here)
    def _():
        totals[DQ, :, here] += stage_a[DQ, side]

    @pl.when(s_here)
    def _():
        for kind in (DK, DV):
            totals[kind, :, here] += stage_a[kind, side]

    @pl.when(led)
    def _():
        for i in range(2):
            arrive(2 - lead + i, other)

    for i in range(2):
        rest_copies[i].wait_recv()

    @pl.when(side == 1)
    def _():
        query_role(1, inbox[K, other], inbox[V, other])
        query_role(0, side_in[0], side_in[1])

    @pl.when(side == 0)
    def _():
        key_role(0, inbox[Q, other], inbox[G, other])
        key_role(1, side_in[0], side_in[1])

    def taken(kind, slot, p):
        away = side != p
        if kind == DQ:
            if slot == 0:
                return (line > 0) & jnp.where(is_main & (core == 1), away, True)
            return (line == 3) & away
        if slot == 0:
            return (line < 3) & jnp.where(is_main & first_core, away, True)
        return (line == 0) & away

    def take(kind, slot, p, r):
        ref = ret.at[kind, slot, p, part(r)]
        remote(ref, ref, side_send.at[0], ret_recv.at[kind, slot, p, r], other).wait_recv()
        at = slice(r * rp, (r + 1) * rp)
        cols = slice(lane * p, lane * (p + 1))
        totals[kind, at, cols] += ret[kind, slot, p, at]

    def collect(r):
        for slot in (1, 0):
            for kinds in ((DQ,), (DK, DV)):
                for p in range(pairs):

                    @pl.when(taken(kinds[0], slot, p))
                    def _():
                        for kind in kinds:
                            take(kind, slot, p, r)

    def to_head(source, target_ref, n, target):
        return pltpu.make_async_remote_copy(
            src_ref=source,
            dst_ref=target_ref,
            send_sem=reduce_send_sem.at[n],
            recv_sem=reduce_recv_sem.at[n],
            device_id={"head": target},
            device_id_type=MESH,
        )

    def to_core(r, n):
        return to_head(core_send_buf.at[r, n], core_recv_buf.at[r, n], 3 * r + n, core_mate)

    def to_far(r):
        return to_head(far_send_buf.at[r], far_recv_buf.at[r], 3 * r + 2, far_mate)

    for r in range(parts):
        collect(r)
        at = slice(r * rp, (r + 1) * rp)
        if r == 0:
            for copy in weight_copies:
                copy.wait()
        final = [totals[i, at].astype(jnp.bfloat16) for i in range(3)]

        def project(target):
            cols = pl.ds(pl.multiple_of(target * out_width, out_width), out_width)
            return sum(dot(final[i], weights[i, :, cols]) for i in range(3))

        core_send_buf[r, 0] = project(2 * (1 - far) + (1 - core))
        to_core(r, 0).start()
        far_send_buf[r] = project(far_mate)
        to_core(r, 0).wait_recv()
        far_send_buf[r] += core_recv_buf[r, 0]
        to_far(r).start()
        core_send_buf[r, 1] = project(core_mate)
        to_core(r, 1).start()
        own_part[at] = project(head)

    for r in range(parts):
        at = slice(r * rp, (r + 1) * rp)
        to_core(r, 1).wait_recv()
        own_part[at] += core_recv_buf[r, 1]
    for r in range(parts):
        at = slice(r * rp, (r + 1) * rp)
        to_far(r).wait_recv()
        out[at] = (own_part[at] + far_recv_buf[r]).astype(out.dtype)

    for r in range(parts):
        to_core(r, 0).wait_send()
        to_core(r, 1).wait_send()
        to_far(r).wait_send()
    for cond, copies in pending:
        if cond is None:
            for copy in copies:
                copy.wait_send()
        else:

            @pl.when(cond)
            def _(copies=copies):
                for copy in copies:
                    copy.wait_send()


def routed_form(n_head, queries, keys, values, out_grad, w_query, w_key, w_value):
    rows, width = queries.shape
    model = w_query.shape[1]
    out_width = model // n_head
    pairs = width // (2 * HD)
    lane = 2 * HD
    blocks = 2 * LINES
    parts = 2
    rp = rows // parts
    f32, bf16 = jnp.float32, jnp.bfloat16
    dma = pltpu.SemaphoreType.DMA
    return pl.pallas_call(
        functools.partial(routed_kernel, parts),
        out_shape=jax.ShapeDtypeStruct((rows, out_width), bf16),
        in_specs=[pl.BlockSpec(memory_space=pl.ANY)] * 7,
        out_specs=pl.BlockSpec(memory_space=pltpu.VMEM),
        scratch_shapes=[
            pltpu.VMEM((4, rows, width), bf16),
            pltpu.VMEM((4, pairs, rows, lane), f32),
            pltpu.VMEM((4, blocks, rows, lane), f32),
            pltpu.VMEM((2, rows, lane), f32),
            pltpu.VMEM((2, 4, rows, lane), bf16),
            pltpu.VMEM((2, 4, 2 * rows, lane), bf16),
            pltpu.VMEM((2, parts, 4 * rp, lane), bf16),
            pltpu.VMEM((2, parts, 2, 4 * rp, lane), bf16),
            pltpu.VMEM((2, parts, 4 * rp, lane), f32),
            pltpu.VMEM((2, 4, rows, lane), f32),
            pltpu.VMEM((3, 2, rows, lane), f32),
            pltpu.VMEM((3, 2, pairs, rows, lane), f32),
            pltpu.VMEM((3, width, model), bf16),
            pltpu.VMEM((3, rows, width), f32),
            pltpu.VMEM((rows, out_width), f32),
            pltpu.VMEM((parts, 2, rp, out_width), f32),
            pltpu.VMEM((parts, 2, rp, out_width), f32),
            pltpu.VMEM((parts, rp, out_width), f32),
            pltpu.VMEM((parts, rp, out_width), f32),
            dma((4,)),
            dma((3,)),
            dma((2, pairs, parts)),
            dma((2, pairs)),
            dma((2, pairs)),
            dma((6,)),
            dma((4, blocks, parts)),
            dma((2,)),
            dma((3, 2, pairs, parts)),
            dma((2, 4, parts)),
            dma((2, 4, parts)),
            dma((3, 2, parts)),
            dma((3 * parts,)),
            dma((3 * parts,)),
        ],
        compiler_params=pltpu.CompilerParams(collective_id=0, has_side_effects=True),
    )(keys, values, queries, out_grad, w_query, w_key, w_value)


def solution(mesh):
    placed = (
        P("seq", "head"),
        P("seq", "head"),
        P("seq", "head"),
        P("seq", "head"),
        P("head", None),
        P("head", None),
        P("head", None),
    )
    n_seq, n_head = mesh.shape["seq"], mesh.shape["head"]

    def per_device(queries, *rest):
        if n_seq == 2 * LINES and n_head == 4 and queries.shape[1] == 4 * HD:
            return routed_form(n_head, queries, *rest)
        return on_device(queries, *rest)

    return jax.shard_map(
        per_device, mesh=mesh, in_specs=placed, out_specs=P("seq", "head"), check_vma=False
    )
```

```python
import functools

import jax
import jax.numpy as jnp
import numpy as np
from jax import lax
from jax.experimental import pallas as pl
from jax.experimental.pallas import tpu as pltpu
from jax.sharding import PartitionSpec as P

HD = 64
MESH = pl.DeviceIdType.MESH


def shifted(value, axis, steps):
    count = lax.axis_size(axis)
    leading, last = (max(0, -steps), min(count, count - steps))
    return lax.ppermute(value, axis, [(source, source + steps) for source in range(leading, last)])


def pair_tables(width):
    first, second = np.triu_indices(width)
    count = first.shape[0]
    select_first = np.zeros((width, count), np.float32)
    select_second = np.zeros((width, count), np.float32)
    select_first[first, np.arange(count)] = 1.0
    select_second[second, np.arange(count)] = 1.0
    scaling = np.where(first == second, 1.0, np.sqrt(2.0)) / width
    return (select_first, select_second, scaling.astype(np.float32))


def expand_features(inputs, pick_first, pick_second, scaling):
    first = jnp.dot(inputs, pick_first, preferred_element_type=jnp.bfloat16)
    second = jnp.dot(inputs, pick_second, preferred_element_type=jnp.bfloat16)
    feats = (first.astype(jnp.float32) * second.astype(jnp.float32) * scaling).astype(jnp.bfloat16)
    return (first, second, feats)


def chain_back(first, second, dphi, back_first, back_second, scaling):
    scaled = dphi * scaling
    left = scaled * second.astype(jnp.float32)
    right = scaled * first.astype(jnp.float32)
    return jnp.dot(
        left, back_first, precision=lax.Precision.HIGHEST, preferred_element_type=jnp.float32
    ) + jnp.dot(
        right, back_second, precision=lax.Precision.HIGHEST, preferred_element_type=jnp.float32
    )


def on_device(queries, keys, values, out_grad, w_query, w_key, w_value):
    count_rows = queries.shape[0]
    head_count = queries.shape[1] // HD
    select_first, select_second, scale_np = pair_tables(HD)
    pick_first = jnp.asarray(select_first, jnp.bfloat16)
    pick_second = jnp.asarray(select_second, jnp.bfloat16)
    back_first = jnp.asarray(select_first.T, jnp.float32)
    back_second = jnp.asarray(select_second.T, jnp.float32)
    scaling = jnp.asarray(scale_np, jnp.float32)
    feat_count = scale_np.shape[0]
    query_heads = queries.reshape(count_rows, head_count, HD)
    key_heads = keys.reshape(count_rows, head_count, HD)
    value_heads = values.reshape(count_rows, head_count, HD)
    grad_heads = out_grad.reshape(count_rows, head_count, HD)
    query_expanded = []
    key_expanded = []
    kv_parts = []
    grad_parts = []
    for number in range(head_count):
        query_set = expand_features(query_heads[:, number], pick_first, pick_second, scaling)
        key_set = expand_features(key_heads[:, number], pick_first, pick_second, scaling)
        query_expanded.append(query_set)
        key_expanded.append(key_set)
        kv_parts.append(
            jnp.einsum(
                "tf,td->fd", key_set[2], value_heads[:, number], preferred_element_type=jnp.float32
            )
        )
        grad_parts.append(
            jnp.einsum(
                "tf,td->fd", query_set[2], grad_heads[:, number], preferred_element_type=jnp.float32
            )
        )
    kv_local = jnp.stack(kv_parts, 1).reshape(feat_count, head_count * HD)
    grad_local = jnp.stack(grad_parts, 1).reshape(feat_count, head_count * HD)
    rounds = (lax.axis_size("seq") - 1).bit_length()
    kv_running = kv_local
    grad_running = grad_local
    for level in range(rounds):
        kv_running = kv_running + shifted(kv_running, "seq", 1 << level)
        grad_running = grad_running + shifted(grad_running, "seq", -(1 << level))
    kv_before = kv_running - kv_local
    grad_after = grad_running - grad_local
    kv_before = kv_before.astype(jnp.bfloat16).reshape(feat_count, head_count, HD)
    grad_after = grad_after.astype(jnp.bfloat16).reshape(feat_count, head_count, HD)
    causal = lax.broadcasted_iota(jnp.int32, (count_rows, count_rows), 0) >= lax.broadcasted_iota(
        jnp.int32, (count_rows, count_rows), 1
    )
    scores = jnp.einsum("thd,shd->hts", query_heads, key_heads, preferred_element_type=jnp.float32)
    products = jnp.einsum(
        "thd,shd->hts", grad_heads, value_heads, preferred_element_type=jnp.float32
    )
    attn = jnp.where(causal, (scores / HD) ** 2, 0.0).astype(jnp.bfloat16)
    pgrad = jnp.where(causal, 2.0 * scores * products / (HD * HD), 0.0).astype(jnp.bfloat16)
    query_local = jnp.einsum("hts,shd->thd", pgrad, key_heads, preferred_element_type=jnp.float32)
    key_local = jnp.einsum("hts,thd->shd", pgrad, query_heads, preferred_element_type=jnp.float32)
    value_local = jnp.einsum("hts,thd->shd", attn, grad_heads, preferred_element_type=jnp.float32)
    query_out = []
    key_out = []
    value_out = []
    for number in range(head_count):
        qfirst, qsecond, query_feat = query_expanded[number]
        kfirst, ksecond, key_feat = key_expanded[number]
        dfq = jnp.einsum(
            "td,fd->tf",
            grad_heads[:, number],
            kv_before[:, number],
            preferred_element_type=jnp.float32,
        )
        dfk = jnp.einsum(
            "td,fd->tf",
            value_heads[:, number],
            grad_after[:, number],
            preferred_element_type=jnp.float32,
        )
        query_out.append(
            query_local[:, number]
            + chain_back(qfirst, qsecond, dfq, back_first, back_second, scaling)
        )
        key_out.append(
            key_local[:, number]
            + chain_back(kfirst, ksecond, dfk, back_first, back_second, scaling)
        )
        value_out.append(
            value_local[:, number]
            + jnp.einsum(
                "tf,fd->td", key_feat, grad_after[:, number], preferred_element_type=jnp.float32
            )
        )
    query_grad = jnp.stack(query_out, 1).astype(jnp.bfloat16).reshape(count_rows, head_count * HD)
    key_grad = jnp.stack(key_out, 1).astype(jnp.bfloat16).reshape(count_rows, head_count * HD)
    value_grad = jnp.stack(value_out, 1).astype(jnp.bfloat16).reshape(count_rows, head_count * HD)
    partial_sum = jnp.dot(query_grad, w_query, preferred_element_type=jnp.float32)
    partial_sum = partial_sum + jnp.dot(key_grad, w_key, preferred_element_type=jnp.float32)
    partial_sum = partial_sum + jnp.dot(value_grad, w_value, preferred_element_type=jnp.float32)
    return lax.psum_scatter(partial_sum, "head", scatter_dimension=1, tiled=True).astype(
        jnp.bfloat16
    )


def masked(block):
    lanes = lax.broadcasted_iota(jnp.int32, block.shape, 1)
    low = jnp.where(lanes < HD, block, 0.0).astype(jnp.bfloat16)
    high = jnp.where(lanes >= HD, block, 0.0).astype(jnp.bfloat16)
    return low, high


def stacked(block):
    return jnp.concatenate(masked(block), axis=0)


def rows_dot(left, right):
    return lax.dot_general(
        left, right, (((1,), (1,)), ((), ())), preferred_element_type=jnp.float32
    )


def dot(left, right):
    return jnp.dot(left, right, preferred_element_type=jnp.float32)


def pgrad_of(scores, products):
    return scores * products * (2.0 / (HD * HD))


def attn_of(scores):
    scaled = scores * (1.0 / HD)
    return scaled * scaled


K, V, Q, G = range(4)
DQ, DK, DV = range(3)
LINES = 4


def routed_kernel(
    parts,
    k_hbm,
    v_hbm,
    q_hbm,
    g_hbm,
    wq_hbm,
    wk_hbm,
    wv_hbm,
    out,
    own,
    mine,
    inbox,
    plain_r,
    stk_r,
    plain_m,
    stk_m,
    stage_m,
    stage_r,
    stage_a,
    stage_o,
    ret,
    weights,
    totals,
    own_part,
    core_send_buf,
    core_recv_buf,
    far_send_buf,
    far_recv_buf,
    own_sem,
    weight_sem,
    mover_send,
    far_send,
    near_send,
    side_send,
    in_recv,
    ret_recv,
    ret_send_m,
    ret_send_r,
    ret_send_a,
    ret_send_o,
    reduce_send_sem,
    reduce_recv_sem,
):
    unused, rows, width = own.shape
    pairs = width // (2 * HD)
    lane = 2 * HD
    rp = rows // parts
    me = lax.axis_index("seq")
    line, side = me // 2, me % 2
    other = 2 * line + (1 - side)
    head = lax.axis_index("head")
    far, core = head // 2, head % 2
    core_mate = 2 * far + (1 - core)
    far_mate = 2 * (1 - far) + core
    out_width = out.shape[1]
    first_core = core == 0

    site = 1 + core
    is_main = line == site
    base_m = jnp.where(first_core, 4, 0)
    base_r = 4 - base_m
    is_mover = jnp.where(first_core, line >= 2, line < 2)
    is_far = line == 3 * core
    inner = (line == 1) | (line == 2)
    outer = jnp.logical_not(inner)
    near_target = jnp.where(line == 1, 0, 3)
    t_line = jnp.where(line < 2, 1, 3)
    s_line = t_line - 1
    skips = line % 2 != core
    mover_a = jnp.where(first_core, Q, K)
    resident_c = Q - mover_a
    has_up, has_down = line < LINES - 1, line > 0

    own_copies = [
        pltpu.make_async_copy(source, own.at[i], own_sem.at[i])
        for i, source in enumerate((k_hbm, v_hbm, q_hbm, g_hbm))
    ]
    for copy in own_copies:
        copy.start()

    barrier = pltpu.get_barrier_semaphore()

    def greet(target):
        pl.semaphore_signal(barrier, inc=1, device_id=target, device_id_type=MESH)

    greet({"seq": other})
    greet({"head": core_mate})
    greet({"head": far_mate})
    for cond, there in ((has_up, line + 1), (has_down, line - 1), (skips, 4 - 2 * core - line)):

        @pl.when(cond)
        def _(there=there):
            for p in range(2):
                greet({"seq": 2 * there + p})

    weight_copies = [
        pltpu.make_async_copy(source, weights.at[i], weight_sem.at[i])
        for i, source in enumerate((wq_hbm, wk_hbm, wv_hbm))
    ]
    for copy in weight_copies:
        copy.start()
    for which, copy in enumerate(own_copies):
        copy.wait()
        for p in range(pairs):
            mine[which, p] = own[which, :, lane * p : lane * (p + 1)].astype(jnp.float32)
        inbox[which, me] = mine[which, side]

    pl.semaphore_wait(
        barrier,
        3
        + 2
        * (
            has_up.astype(jnp.int32)
            + has_down.astype(jnp.int32)
            + skips.astype(jnp.int32)
        ),
    )

    def remote(source, target_ref, send, recv, target):
        return pltpu.make_async_remote_copy(
            src_ref=source,
            dst_ref=target_ref,
            send_sem=send,
            recv_sem=recv,
            device_id={"seq": target},
            device_id_type=MESH,
        )

    def part(r):
        return pl.ds(r * rp, rp)

    def mover_copy(i, p, r):
        w = mover_a + i
        return remote(
            mine.at[w, p, part(r)],
            inbox.at[w, me, part(r)],
            mover_send.at[i, p, r],
            in_recv.at[w, me, r],
            2 * site + p,
        )

    def whole_copy(w, p, send, target):
        return remote(mine.at[w, p], inbox.at[w, me], send, in_recv.at[w, me, 0], target)

    def far_copy(i, p):
        return whole_copy(resident_c + i, p, far_send.at[i, p], 2 * site + p)

    def near_copy(i, p):
        return whole_copy(near_a + i, p, near_send.at[i, p], 2 * near_target + p)

    lead = 2 * side
    near_a = jnp.where(line % 2 == 1, Q, K)
    needed = jnp.where(outer, 2 * (line // 2), resident_c)
    plain = inner & jnp.logical_not(is_main)
    sent = jnp.where(plain, lead, needed)
    got = jnp.where(plain, 2 - lead, needed)
    leads, led = sent != lead, got != 2 - lead

    def exchange_copy(i):
        return whole_copy(sent + i, 1 - side, side_send.at[i], other)

    def lead_copy(i):
        return whole_copy(lead + i, 1 - side, side_send.at[4 + i], other)

    pending = []

    def launch(cond, copies, again=False):
        if not again:
            pending.append((cond, copies))
        if cond is None:
            for copy in copies:
                copy.start()
        else:

            @pl.when(cond)
            def _():
                for copy in copies:
                    copy.start()

    crossing = [(i, p) for p in range(pairs) for i in range(2)]
    movers_of = [[mover_copy(i, p, r) for i, p in crossing] for r in range(parts)]
    far_copies = [far_copy(i, p) for i, p in crossing]
    near_copies = [near_copy(i, p) for i, p in crossing]
    exchanges = [exchange_copy(i) for i in range(2)]
    lead_copies = [lead_copy(i) for i in range(2)]

    launch(is_mover, movers_of[0])
    launch(is_far, far_copies)
    launch(jnp.logical_not(plain), exchanges)
    launch(inner, near_copies)

    def arrive(w, b, r=None):
        ref = inbox.at[w, b] if r is None else inbox.at[w, b, part(r)]
        sem = in_recv.at[w, b, 0 if r is None else r]
        remote(ref, ref, side_send.at[0], sem, other).wait_recv()

    def columns(p):
        return pl.ds(pl.multiple_of(p * lane, lane), lane)

    def diagonal(p):
        cols = columns(p)
        t = lax.broadcasted_iota(jnp.int32, (rows, 2 * rows), 0)
        s = lax.broadcasted_iota(jnp.int32, (rows, 2 * rows), 1) % rows
        k2, v2 = stacked(mine[K, p]), stacked(mine[V, p])
        weight = pgrad_of(rows_dot(own[Q, :, cols], k2), rows_dot(own[G, :, cols], v2))
        weight = jnp.where(t >= s, weight, 0.0)
        totals[DQ, :, cols] = dot(weight.astype(jnp.bfloat16), k2)
        q2, g2 = stacked(mine[Q, p]), stacked(mine[G, p])
        scores = rows_dot(own[K, :, cols], q2)
        weight = pgrad_of(scores, rows_dot(own[V, :, cols], g2))
        weight = jnp.where(s >= t, weight, 0.0)
        attn = jnp.where(s >= t, attn_of(scores), 0.0)
        totals[DK, :, cols] = dot(weight.astype(jnp.bfloat16), q2)
        totals[DV, :, cols] = dot(attn.astype(jnp.bfloat16), g2)

    for p in range(pairs):
        diagonal(p)

    for r in range(1, parts):
        launch(is_mover, movers_of[r])
    launch(plain, exchanges)
    launch(leads, lead_copies)
    for i in range(2):
        arrive(got + i, other)

    def give(kind, slot, source, r, send, target):
        return remote(
            source, ret.at[kind, slot, side, part(r)], send, ret_recv.at[kind, slot, side, r], target
        )

    here = columns(side)

    def own_pair():
        even, odd = 2 * line, 2 * line + 1
        k, v, q, g = inbox[K, even], inbox[V, even], inbox[Q, odd], inbox[G, odd]
        k2, v2 = stacked(k), stacked(v)
        weight = pgrad_of(
            rows_dot(q.astype(jnp.bfloat16), k2), rows_dot(g.astype(jnp.bfloat16), v2)
        )
        stage_o[DQ] = dot(weight.astype(jnp.bfloat16), k2)
        q2, g2 = stacked(q), stacked(g)
        scores = rows_dot(k.astype(jnp.bfloat16), q2)
        weight = pgrad_of(scores, rows_dot(v.astype(jnp.bfloat16), g2))
        stage_o[DK] = dot(weight.astype(jnp.bfloat16), q2)
        stage_o[DV] = dot(attn_of(scores).astype(jnp.bfloat16), g2)

        @pl.when(side == 1)
        def _():
            totals[DQ, :, here] += stage_o[DQ]

        @pl.when(side == 0)
        def _():
            for kind in (DK, DV):
                totals[kind, :, here] += stage_o[kind]

    early = jnp.logical_not(led | plain)
    joins_k, joins_q = early & (side == 1), early & (side == 0)
    pl.when(early)(own_pair)
    every = [(j, r) for r in range(parts) for j in range(2)]

    def mover_give(i, j, r):
        kind = jnp.where(first_core, DQ, DK) + i
        return give(
            kind,
            0,
            stage_m.at[i, r, pl.ds(j * rp, rp)],
            r,
            ret_send_m.at[i, j, r],
            base_m + j,
        )

    def resident_give(i, j, r):
        kind = jnp.where(first_core, DK, DQ) + i
        return give(
            kind, 0, stage_r.at[i, j, part(r)], r, ret_send_r.at[i, j, r], base_r + j
        )

    far_j = 2 * core
    near_j = 2 * (1 - core)
    flat = 4 * rp

    @pl.when(is_main)
    def _():
        for j in range(2):
            for i in range(2):
                arrive(resident_c + i, base_r + far_j + j)
        for j in range(4):
            for i in range(2):
                block = inbox[resident_c + i, base_r + j]
                plain_r[i, j] = block.astype(jnp.bfloat16)
                stk_r[i, j] = stacked(block)

    def resident_major(both, q):
        at = slice(q * rp, (q + 1) * rp)
        left_c = plain_r[0, :, at].reshape(flat, lane)
        left_d = plain_r[1, :, at].reshape(flat, lane)
        grad_c = grad_d = None
        for r in range(parts):
            for h in range(2):
                a2, b2 = stk_m[0, r, h], stk_m[1, r, h]
                scores = rows_dot(left_c, a2)
                products = rows_dot(left_d, b2)
                term = dot(pgrad_of(scores, products).astype(jnp.bfloat16), a2)
                grad_c = term if grad_c is None else grad_c + term
                if both:
                    term = dot(attn_of(scores).astype(jnp.bfloat16), b2)
                    grad_d = term if grad_d is None else grad_d + term
        stage_r[0, :, at] = grad_c.reshape(4, rp, lane)
        if both:
            stage_r[1, :, at] = grad_d.reshape(4, rp, lane)

    def join_resident(kinds, block, q):
        at = slice(q * rp, (q + 1) * rp)
        for i, kind in enumerate(kinds):
            stage_r[i, near_j + block, at] += stage_o[kind, at]

    def resident_gives(arrays, q):
        return [resident_give(i, far_j + j, q) for j in range(2) for i in arrays] + [
            resident_give(i, near_j + 1 - side, q) for i in arrays
        ]

    for r in range(parts):

        @pl.when(is_main)
        def _(r=r):
            for j in range(4):
                for i in range(2):
                    arrive(mover_a + i, base_m + j, r)
            for j in range(4):
                for i in range(2):
                    block = inbox[mover_a + i, base_m + j, part(r)]
                    low, high = masked(block)
                    at = slice(j * rp, (j + 1) * rp)
                    plain_m[i, r, at] = block.astype(jnp.bfloat16)
                    stk_m[i, r, 0, at] = low
                    stk_m[i, r, 1, at] = high

        def mover_major(both, r):
            grad_a = grad_b = None
            for j in range(4):
                scores = rows_dot(plain_m[0, r], stk_r[0, j])
                products = rows_dot(plain_m[1, r], stk_r[1, j])
                term = dot(pgrad_of(scores, products).astype(jnp.bfloat16), stk_r[0, j])
                grad_a = term if grad_a is None else grad_a + term
                if both:
                    term = dot(attn_of(scores).astype(jnp.bfloat16), stk_r[1, j])
                    grad_b = term if grad_b is None else grad_b + term
            stage_m[0, r] = grad_a
            if both:
                stage_m[1, r] = grad_b

        if r == parts - 1:
            for q in range(parts):
                pl.when(is_main & first_core)(lambda: resident_major(True, q))
                pl.when(is_main & joins_k)(lambda: join_resident((DK, DV), 0, q))
                launch(is_main & first_core, resident_gives((0, 1), q))
            for n in range(parts):
                pl.when(is_main & first_core)(lambda: mover_major(False, n))
                launch(is_main & first_core, [mover_give(0, j, n) for j in range(4)])
        pl.when(is_main & (core == 1))(lambda: mover_major(True, r))
        launch(is_main & (core == 1), [mover_give(i, j, r) for j in range(4) for i in range(2)])

    for q in range(parts):
        pl.when(is_main & (core == 1))(lambda: resident_major(False, q))
        pl.when(is_main & joins_q)(lambda: join_resident((DQ,), 1, q))
        launch(is_main & (core == 1), resident_gives((0,), q))

    @pl.when(is_main & first_core)
    def _():
        totals[DK, :, here] += stage_r[0, near_j + side]
        totals[DV, :, here] += stage_r[1, near_j + side]

    @pl.when(is_main & (core == 1))
    def _():
        totals[DQ, :, here] += stage_r[0, near_j + side]

    @pl.when(outer)
    def _():
        from_line = jnp.where(line == 0, 1, 2)
        for j in range(2):
            for i in range(2):
                arrive(Q - needed + i, 2 * from_line + j)

    def pair_part(w, at_line, j):
        return inbox[w, 2 * at_line + j]

    @pl.when(outer)
    def _():
        k_blocks = [pair_part(K, s_line, j) for j in range(2)]
        v_blocks = [pair_part(V, s_line, j) for j in range(2)]
        k2 = jnp.concatenate([stacked(b) for b in k_blocks], axis=0)
        v2 = jnp.concatenate([stacked(b) for b in v_blocks], axis=0)
        for j in range(2):
            q = pair_part(Q, t_line, j).astype(jnp.bfloat16)
            g = pair_part(G, t_line, j).astype(jnp.bfloat16)
            weight = pgrad_of(rows_dot(q, k2), rows_dot(g, v2))
            stage_a[DQ, j] = dot(weight.astype(jnp.bfloat16), k2)
        q2 = jnp.concatenate([stacked(pair_part(Q, t_line, j)) for j in range(2)], axis=0)
        g2 = jnp.concatenate([stacked(pair_part(G, t_line, j)) for j in range(2)], axis=0)
        for j in range(2):
            scores = rows_dot(k_blocks[j].astype(jnp.bfloat16), q2)
            products = rows_dot(v_blocks[j].astype(jnp.bfloat16), g2)
            stage_a[DK, j] = dot(pgrad_of(scores, products).astype(jnp.bfloat16), q2)
            stage_a[DV, j] = dot(attn_of(scores).astype(jnp.bfloat16), g2)

    @pl.when(outer & joins_k)
    def _():
        for kind in (DK, DV):
            stage_a[kind, 0] += stage_o[kind]

    @pl.when(outer & joins_q)
    def _():
        stage_a[DQ, 1] += stage_o[DQ]

    def pair_give(kind, j, r, target):
        slot = jnp.where(target == other, 1, 0)
        return give(kind, slot, stage_a.at[kind, j, part(r)], r, ret_send_a.at[kind, j, r], target)

    def pair_gives(kinds, j, target):
        return [pair_give(kind, j, r, target) for r in range(parts) for kind in kinds]

    t_here, s_here = line == 3, line == 0
    launch(s_here, [c for j in range(2) for c in pair_gives((DQ,), j, 2 * t_line + j)])
    launch(s_here, pair_gives((DK, DV), 1 - side, other))
    launch(t_here, [c for j in range(2) for c in pair_gives((DK, DV), j, 2 * s_line + j)])
    launch(t_here, pair_gives((DQ,), 1 - side, other))

    @pl.when(t_here)
    def _():
        totals[DQ, :, here] += stage_a[DQ, side]

    @pl.when(s_here)
    def _():
        for kind in (DK, DV):
            totals[kind, :, here] += stage_a[kind, side]

    @pl.when(led)
    def _():
        for i in range(2):
            arrive(2 - lead + i, other)

    late = led | plain
    pl.when(late)(own_pair)

    def own_give(kind, r):
        return give(kind, 2, stage_o.at[kind, part(r)], r, ret_send_o.at[kind, r], other)

    launch(late & (side == 0), [own_give(DQ, r) for r in range(parts)])
    launch(late & (side == 1), [own_give(kind, r) for r in range(parts) for kind in (DK, DV)])

    def taken(kind, slot, p):
        away = side != p
        if slot == 2:
            wanted = side == (1 if kind == DQ else 0)
            other_needed = needed == (Q if kind == DQ else K)
            return away & wanted & (plain | jnp.logical_not(other_needed))
        if kind == DQ:
            if slot == 0:
                return (line > 0) & jnp.where(is_main & (core == 1), away, True)
            return (line == 3) & away
        if slot == 0:
            return (line < 3) & jnp.where(is_main & first_core, away, True)
        return (line == 0) & away

    def take(kind, slot, p, r):
        ref = ret.at[kind, slot, p, part(r)]
        remote(ref, ref, side_send.at[0], ret_recv.at[kind, slot, p, r], other).wait_recv()
        at = slice(r * rp, (r + 1) * rp)
        cols = slice(lane * p, lane * (p + 1))
        totals[kind, at, cols] += ret[kind, slot, p, at]

    def collect(r):
        for slot in (2, 1, 0):
            for kinds in ((DQ,), (DK, DV)):
                for p in range(pairs):

                    @pl.when(taken(kinds[0], slot, p))
                    def _():
                        for kind in kinds:
                            take(kind, slot, p, r)

    def to_head(source, target_ref, n, target):
        return pltpu.make_async_remote_copy(
            src_ref=source,
            dst_ref=target_ref,
            send_sem=reduce_send_sem.at[n],
            recv_sem=reduce_recv_sem.at[n],
            device_id={"head": target},
            device_id_type=MESH,
        )

    def to_core(r, n):
        return to_head(core_send_buf.at[r, n], core_recv_buf.at[r, n], 3 * r + n, core_mate)

    def to_far(r):
        return to_head(far_send_buf.at[r], far_recv_buf.at[r], 3 * r + 2, far_mate)

    for r in range(parts):
        collect(r)
        at = slice(r * rp, (r + 1) * rp)
        if r == 0:
            for copy in weight_copies:
                copy.wait()
        final = [totals[i, at].astype(jnp.bfloat16) for i in range(3)]

        def project(target):
            cols = pl.ds(pl.multiple_of(target * out_width, out_width), out_width)
            return sum(dot(final[i], weights[i, :, cols]) for i in range(3))

        core_send_buf[r, 0] = project(2 * (1 - far) + (1 - core))
        to_core(r, 0).start()
        far_send_buf[r] = project(far_mate)
        to_core(r, 0).wait_recv()
        far_send_buf[r] += core_recv_buf[r, 0]
        to_far(r).start()
        core_send_buf[r, 1] = project(core_mate)
        to_core(r, 1).start()
        own_part[at] = project(head)

    for r in range(parts):
        at = slice(r * rp, (r + 1) * rp)
        to_core(r, 1).wait_recv()
        own_part[at] += core_recv_buf[r, 1]
    for r in range(parts):
        at = slice(r * rp, (r + 1) * rp)
        to_far(r).wait_recv()
        out[at] = (own_part[at] + far_recv_buf[r]).astype(out.dtype)

    for r in range(parts):
        to_core(r, 0).wait_send()
        to_core(r, 1).wait_send()
        to_far(r).wait_send()
    for cond, copies in pending:
        if cond is None:
            for copy in copies:
                copy.wait_send()
        else:

            @pl.when(cond)
            def _(copies=copies):
                for copy in copies:
                    copy.wait_send()


def routed_form(n_head, queries, keys, values, out_grad, w_query, w_key, w_value):
    rows, width = queries.shape
    model = w_query.shape[1]
    out_width = model // n_head
    pairs = width // (2 * HD)
    lane = 2 * HD
    blocks = 2 * LINES
    parts = 2
    rp = rows // parts
    f32, bf16 = jnp.float32, jnp.bfloat16
    dma = pltpu.SemaphoreType.DMA
    return pl.pallas_call(
        functools.partial(routed_kernel, parts),
        out_shape=jax.ShapeDtypeStruct((rows, out_width), bf16),
        in_specs=[pl.BlockSpec(memory_space=pl.ANY)] * 7,
        out_specs=pl.BlockSpec(memory_space=pltpu.VMEM),
        scratch_shapes=[
            pltpu.VMEM((4, rows, width), bf16),
            pltpu.VMEM((4, pairs, rows, lane), f32),
            pltpu.VMEM((4, blocks, rows, lane), f32),
            pltpu.VMEM((2, 4, rows, lane), bf16),
            pltpu.VMEM((2, 4, 2 * rows, lane), bf16),
            pltpu.VMEM((2, parts, 4 * rp, lane), bf16),
            pltpu.VMEM((2, parts, 2, 4 * rp, lane), bf16),
            pltpu.VMEM((2, parts, 4 * rp, lane), f32),
            pltpu.VMEM((2, 4, rows, lane), f32),
            pltpu.VMEM((3, 2, rows, lane), f32),
            pltpu.VMEM((3, rows, lane), f32),
            pltpu.VMEM((3, 3, pairs, rows, lane), f32),
            pltpu.VMEM((3, width, model), bf16),
            pltpu.VMEM((3, rows, width), f32),
            pltpu.VMEM((rows, out_width), f32),
            pltpu.VMEM((parts, 2, rp, out_width), f32),
            pltpu.VMEM((parts, 2, rp, out_width), f32),
            pltpu.VMEM((parts, rp, out_width), f32),
            pltpu.VMEM((parts, rp, out_width), f32),
            dma((4,)),
            dma((3,)),
            dma((2, pairs, parts)),
            dma((2, pairs)),
            dma((2, pairs)),
            dma((6,)),
            dma((4, blocks, parts)),
            dma((3, 3, pairs, parts)),
            dma((2, 4, parts)),
            dma((2, 4, parts)),
            dma((3, 2, parts)),
            dma((3, parts)),
            dma((3 * parts,)),
            dma((3 * parts,)),
        ],
        compiler_params=pltpu.CompilerParams(collective_id=0, has_side_effects=True),
    )(keys, values, queries, out_grad, w_query, w_key, w_value)


def solution(mesh):
    placed = (
        P("seq", "head"),
        P("seq", "head"),
        P("seq", "head"),
        P("seq", "head"),
        P("head", None),
        P("head", None),
        P("head", None),
    )
    n_seq, n_head = mesh.shape["seq"], mesh.shape["head"]

    def per_device(queries, *rest):
        if n_seq == 2 * LINES and n_head == 4 and queries.shape[1] == 4 * HD:
            return routed_form(n_head, queries, *rest)
        return on_device(queries, *rest)

    return jax.shard_map(
        per_device, mesh=mesh, in_specs=placed, out_specs=P("seq", "head"), check_vma=False
    )
```

```python
import functools

import jax
import jax.numpy as jnp
import numpy as np
from jax import lax
from jax.experimental import pallas as pl
from jax.experimental.pallas import tpu as pltpu
from jax.sharding import PartitionSpec as P

HD = 64
MESH = pl.DeviceIdType.MESH


def shifted(value, axis, steps):
    count = lax.axis_size(axis)
    leading, last = (max(0, -steps), min(count, count - steps))
    return lax.ppermute(value, axis, [(source, source + steps) for source in range(leading, last)])


def pair_tables(width):
    first, second = np.triu_indices(width)
    count = first.shape[0]
    select_first = np.zeros((width, count), np.float32)
    select_second = np.zeros((width, count), np.float32)
    select_first[first, np.arange(count)] = 1.0
    select_second[second, np.arange(count)] = 1.0
    scaling = np.where(first == second, 1.0, np.sqrt(2.0)) / width
    return (select_first, select_second, scaling.astype(np.float32))


def expand_features(inputs, pick_first, pick_second, scaling):
    first = jnp.dot(inputs, pick_first, preferred_element_type=jnp.bfloat16)
    second = jnp.dot(inputs, pick_second, preferred_element_type=jnp.bfloat16)
    feats = (first.astype(jnp.float32) * second.astype(jnp.float32) * scaling).astype(jnp.bfloat16)
    return (first, second, feats)


def chain_back(first, second, dphi, back_first, back_second, scaling):
    scaled = dphi * scaling
    left = scaled * second.astype(jnp.float32)
    right = scaled * first.astype(jnp.float32)
    return jnp.dot(
        left, back_first, precision=lax.Precision.HIGHEST, preferred_element_type=jnp.float32
    ) + jnp.dot(
        right, back_second, precision=lax.Precision.HIGHEST, preferred_element_type=jnp.float32
    )


def on_device(queries, keys, values, out_grad, w_query, w_key, w_value):
    count_rows = queries.shape[0]
    head_count = queries.shape[1] // HD
    select_first, select_second, scale_np = pair_tables(HD)
    pick_first = jnp.asarray(select_first, jnp.bfloat16)
    pick_second = jnp.asarray(select_second, jnp.bfloat16)
    back_first = jnp.asarray(select_first.T, jnp.float32)
    back_second = jnp.asarray(select_second.T, jnp.float32)
    scaling = jnp.asarray(scale_np, jnp.float32)
    feat_count = scale_np.shape[0]
    query_heads = queries.reshape(count_rows, head_count, HD)
    key_heads = keys.reshape(count_rows, head_count, HD)
    value_heads = values.reshape(count_rows, head_count, HD)
    grad_heads = out_grad.reshape(count_rows, head_count, HD)
    query_expanded = []
    key_expanded = []
    kv_parts = []
    grad_parts = []
    for number in range(head_count):
        query_set = expand_features(query_heads[:, number], pick_first, pick_second, scaling)
        key_set = expand_features(key_heads[:, number], pick_first, pick_second, scaling)
        query_expanded.append(query_set)
        key_expanded.append(key_set)
        kv_parts.append(
            jnp.einsum(
                "tf,td->fd", key_set[2], value_heads[:, number], preferred_element_type=jnp.float32
            )
        )
        grad_parts.append(
            jnp.einsum(
                "tf,td->fd", query_set[2], grad_heads[:, number], preferred_element_type=jnp.float32
            )
        )
    kv_local = jnp.stack(kv_parts, 1).reshape(feat_count, head_count * HD)
    grad_local = jnp.stack(grad_parts, 1).reshape(feat_count, head_count * HD)
    rounds = (lax.axis_size("seq") - 1).bit_length()
    kv_running = kv_local
    grad_running = grad_local
    for level in range(rounds):
        kv_running = kv_running + shifted(kv_running, "seq", 1 << level)
        grad_running = grad_running + shifted(grad_running, "seq", -(1 << level))
    kv_before = kv_running - kv_local
    grad_after = grad_running - grad_local
    kv_before = kv_before.astype(jnp.bfloat16).reshape(feat_count, head_count, HD)
    grad_after = grad_after.astype(jnp.bfloat16).reshape(feat_count, head_count, HD)
    causal = lax.broadcasted_iota(jnp.int32, (count_rows, count_rows), 0) >= lax.broadcasted_iota(
        jnp.int32, (count_rows, count_rows), 1
    )
    scores = jnp.einsum("thd,shd->hts", query_heads, key_heads, preferred_element_type=jnp.float32)
    products = jnp.einsum(
        "thd,shd->hts", grad_heads, value_heads, preferred_element_type=jnp.float32
    )
    attn = jnp.where(causal, (scores / HD) ** 2, 0.0).astype(jnp.bfloat16)
    pgrad = jnp.where(causal, 2.0 * scores * products / (HD * HD), 0.0).astype(jnp.bfloat16)
    query_local = jnp.einsum("hts,shd->thd", pgrad, key_heads, preferred_element_type=jnp.float32)
    key_local = jnp.einsum("hts,thd->shd", pgrad, query_heads, preferred_element_type=jnp.float32)
    value_local = jnp.einsum("hts,thd->shd", attn, grad_heads, preferred_element_type=jnp.float32)
    query_out = []
    key_out = []
    value_out = []
    for number in range(head_count):
        qfirst, qsecond, query_feat = query_expanded[number]
        kfirst, ksecond, key_feat = key_expanded[number]
        dfq = jnp.einsum(
            "td,fd->tf",
            grad_heads[:, number],
            kv_before[:, number],
            preferred_element_type=jnp.float32,
        )
        dfk = jnp.einsum(
            "td,fd->tf",
            value_heads[:, number],
            grad_after[:, number],
            preferred_element_type=jnp.float32,
        )
        query_out.append(
            query_local[:, number]
            + chain_back(qfirst, qsecond, dfq, back_first, back_second, scaling)
        )
        key_out.append(
            key_local[:, number]
            + chain_back(kfirst, ksecond, dfk, back_first, back_second, scaling)
        )
        value_out.append(
            value_local[:, number]
            + jnp.einsum(
                "tf,fd->td", key_feat, grad_after[:, number], preferred_element_type=jnp.float32
            )
        )
    query_grad = jnp.stack(query_out, 1).astype(jnp.bfloat16).reshape(count_rows, head_count * HD)
    key_grad = jnp.stack(key_out, 1).astype(jnp.bfloat16).reshape(count_rows, head_count * HD)
    value_grad = jnp.stack(value_out, 1).astype(jnp.bfloat16).reshape(count_rows, head_count * HD)
    partial_sum = jnp.dot(query_grad, w_query, preferred_element_type=jnp.float32)
    partial_sum = partial_sum + jnp.dot(key_grad, w_key, preferred_element_type=jnp.float32)
    partial_sum = partial_sum + jnp.dot(value_grad, w_value, preferred_element_type=jnp.float32)
    return lax.psum_scatter(partial_sum, "head", scatter_dimension=1, tiled=True).astype(
        jnp.bfloat16
    )


def masked(block):
    lanes = lax.broadcasted_iota(jnp.int32, block.shape, 1)
    low = jnp.where(lanes < HD, block, 0.0).astype(jnp.bfloat16)
    high = jnp.where(lanes >= HD, block, 0.0).astype(jnp.bfloat16)
    return low, high


def stacked(block):
    return jnp.concatenate(masked(block), axis=0)


def rows_dot(left, right):
    return lax.dot_general(
        left, right, (((1,), (1,)), ((), ())), preferred_element_type=jnp.float32
    )


def dot(left, right):
    return jnp.dot(left, right, preferred_element_type=jnp.float32)


def pgrad_of(scores, products):
    return scores * products * (2.0 / (HD * HD))


def attn_of(scores):
    scaled = scores * (1.0 / HD)
    return scaled * scaled


K, V, Q, G = range(4)
DQ, DK, DV = range(3)
LINES = 4


def routed_kernel(
    parts,
    k_hbm,
    v_hbm,
    q_hbm,
    g_hbm,
    wq_hbm,
    wk_hbm,
    wv_hbm,
    own_out,
    far_out,
    own,
    mine,
    inbox,
    plain_r,
    stk_r,
    plain_m,
    stk_m,
    stage_m,
    stage_r,
    stage_a,
    stage_o,
    ret,
    weights,
    totals,
    own_part,
    core_send_buf,
    core_recv_buf,
    far_send_buf,
    own_sem,
    weight_sem,
    out_sem,
    mover_send,
    far_send,
    near_send,
    side_send,
    in_recv,
    ret_recv,
    ret_send_m,
    ret_send_r,
    ret_send_a,
    ret_send_o,
    reduce_send_sem,
    reduce_recv_sem,
):
    unused, rows, width = own.shape
    pairs = width // (2 * HD)
    lane = 2 * HD
    rp = rows // parts
    me = lax.axis_index("seq")
    line, side = me // 2, me % 2
    other = 2 * line + (1 - side)
    head = lax.axis_index("head")
    far, core = head // 2, head % 2
    core_mate = 2 * far + (1 - core)
    far_mate = 2 * (1 - far) + core
    out_width = own_out.shape[1]
    first_core = core == 0

    site = 1 + core
    is_main = line == site
    base_m = jnp.where(first_core, 4, 0)
    base_r = 4 - base_m
    is_mover = jnp.where(first_core, line >= 2, line < 2)
    is_far = line == 3 * core
    inner = (line == 1) | (line == 2)
    outer = jnp.logical_not(inner)
    near_target = jnp.where(line == 1, 0, 3)
    t_line = jnp.where(line < 2, 1, 3)
    s_line = t_line - 1
    skips = line % 2 != core
    mover_a = jnp.where(first_core, Q, K)
    resident_c = Q - mover_a
    has_up, has_down = line < LINES - 1, line > 0

    own_copies = [
        pltpu.make_async_copy(source, own.at[i], own_sem.at[i])
        for i, source in enumerate((k_hbm, v_hbm, q_hbm, g_hbm))
    ]
    for copy in own_copies:
        copy.start()

    barrier = pltpu.get_barrier_semaphore()

    def greet(target):
        pl.semaphore_signal(barrier, inc=1, device_id=target, device_id_type=MESH)

    greet({"seq": other})
    greet({"head": core_mate})
    greet({"head": far_mate})
    for cond, there in ((has_up, line + 1), (has_down, line - 1), (skips, 4 - 2 * core - line)):

        @pl.when(cond)
        def _(there=there):
            for p in range(2):
                greet({"seq": 2 * there + p})

    weight_copies = [
        pltpu.make_async_copy(source, weights.at[i], weight_sem.at[i])
        for i, source in enumerate((wq_hbm, wk_hbm, wv_hbm))
    ]
    for copy in weight_copies:
        copy.start()
    for which, copy in enumerate(own_copies):
        copy.wait()
        for p in range(pairs):
            mine[which, p] = own[which, :, lane * p : lane * (p + 1)].astype(jnp.float32)
        inbox[which, me] = mine[which, side]

    pl.semaphore_wait(
        barrier,
        3
        + 2
        * (
            has_up.astype(jnp.int32)
            + has_down.astype(jnp.int32)
            + skips.astype(jnp.int32)
        ),
    )

    def remote(source, target_ref, send, recv, target):
        return pltpu.make_async_remote_copy(
            src_ref=source,
            dst_ref=target_ref,
            send_sem=send,
            recv_sem=recv,
            device_id={"seq": target},
            device_id_type=MESH,
        )

    def part(r):
        return pl.ds(r * rp, rp)

    def mover_copy(i, p, r):
        w = mover_a + i
        return remote(
            mine.at[w, p, part(r)],
            inbox.at[w, me, part(r)],
            mover_send.at[i, p, r],
            in_recv.at[w, me, r],
            2 * site + p,
        )

    def whole_copy(w, p, send, target):
        return remote(mine.at[w, p], inbox.at[w, me], send, in_recv.at[w, me, 0], target)

    def far_copy(i, p):
        return whole_copy(resident_c + i, p, far_send.at[i, p], 2 * site + p)

    def near_copy(i, p):
        return whole_copy(near_a + i, p, near_send.at[i, p], 2 * near_target + p)

    lead = 2 * side
    near_a = jnp.where(line % 2 == 1, Q, K)
    needed = jnp.where(outer, 2 * (line // 2), resident_c)
    plain = inner & jnp.logical_not(is_main)
    sent = jnp.where(plain, lead, needed)
    got = jnp.where(plain, 2 - lead, needed)
    leads, led = sent != lead, got != 2 - lead

    def exchange_copy(i):
        return whole_copy(sent + i, 1 - side, side_send.at[i], other)

    def lead_copy(i):
        return whole_copy(lead + i, 1 - side, side_send.at[4 + i], other)

    pending = []

    def launch(cond, copies, again=False):
        if not again:
            pending.append((cond, copies))
        if cond is None:
            for copy in copies:
                copy.start()
        else:

            @pl.when(cond)
            def _():
                for copy in copies:
                    copy.start()

    crossing = [(i, p) for p in range(pairs) for i in range(2)]
    movers_of = [[mover_copy(i, p, r) for i, p in crossing] for r in range(parts)]
    far_copies = [far_copy(i, p) for i, p in crossing]
    near_copies = [near_copy(i, p) for i, p in crossing]
    exchanges = [exchange_copy(i) for i in range(2)]
    lead_copies = [lead_copy(i) for i in range(2)]

    launch(is_mover, movers_of[0])
    launch(is_far, far_copies)
    launch(jnp.logical_not(plain), exchanges)
    launch(inner, near_copies)

    def arrive(w, b, r=None):
        ref = inbox.at[w, b] if r is None else inbox.at[w, b, part(r)]
        sem = in_recv.at[w, b, 0 if r is None else r]
        remote(ref, ref, side_send.at[0], sem, other).wait_recv()

    def columns(p):
        return pl.ds(pl.multiple_of(p * lane, lane), lane)

    def diagonal(p):
        cols = columns(p)
        t = lax.broadcasted_iota(jnp.int32, (rows, 2 * rows), 0)
        s = lax.broadcasted_iota(jnp.int32, (rows, 2 * rows), 1) % rows
        k2, v2 = stacked(mine[K, p]), stacked(mine[V, p])
        weight = pgrad_of(rows_dot(own[Q, :, cols], k2), rows_dot(own[G, :, cols], v2))
        weight = jnp.where(t >= s, weight, 0.0)
        totals[DQ, :, cols] = dot(weight.astype(jnp.bfloat16), k2)
        q2, g2 = stacked(mine[Q, p]), stacked(mine[G, p])
        scores = rows_dot(own[K, :, cols], q2)
        weight = pgrad_of(scores, rows_dot(own[V, :, cols], g2))
        weight = jnp.where(s >= t, weight, 0.0)
        attn = jnp.where(s >= t, attn_of(scores), 0.0)
        totals[DK, :, cols] = dot(weight.astype(jnp.bfloat16), q2)
        totals[DV, :, cols] = dot(attn.astype(jnp.bfloat16), g2)

    for p in range(pairs):
        diagonal(p)

    for r in range(1, parts):
        launch(is_mover, movers_of[r])
    launch(plain, exchanges)
    launch(leads, lead_copies)
    for i in range(2):
        arrive(got + i, other)

    def give(kind, slot, source, r, send, target):
        return remote(
            source, ret.at[kind, slot, side, part(r)], send, ret_recv.at[kind, slot, side, r], target
        )

    here = columns(side)

    def own_pair():
        even, odd = 2 * line, 2 * line + 1
        k, v, q, g = inbox[K, even], inbox[V, even], inbox[Q, odd], inbox[G, odd]
        k2, v2 = stacked(k), stacked(v)
        weight = pgrad_of(
            rows_dot(q.astype(jnp.bfloat16), k2), rows_dot(g.astype(jnp.bfloat16), v2)
        )
        stage_o[DQ] = dot(weight.astype(jnp.bfloat16), k2)
        q2, g2 = stacked(q), stacked(g)
        scores = rows_dot(k.astype(jnp.bfloat16), q2)
        weight = pgrad_of(scores, rows_dot(v.astype(jnp.bfloat16), g2))
        stage_o[DK] = dot(weight.astype(jnp.bfloat16), q2)
        stage_o[DV] = dot(attn_of(scores).astype(jnp.bfloat16), g2)

        @pl.when(side == 1)
        def _():
            totals[DQ, :, here] += stage_o[DQ]

        @pl.when(side == 0)
        def _():
            for kind in (DK, DV):
                totals[kind, :, here] += stage_o[kind]

    early = jnp.logical_not(led | plain)
    joins_k, joins_q = early & (side == 1), early & (side == 0)
    pl.when(early)(own_pair)
    every = [(j, r) for r in range(parts) for j in range(2)]

    def mover_give(i, j, r):
        kind = jnp.where(first_core, DQ, DK) + i
        return give(
            kind,
            0,
            stage_m.at[i, r, pl.ds(j * rp, rp)],
            r,
            ret_send_m.at[i, j, r],
            base_m + j,
        )

    def resident_give(i, j, r):
        kind = jnp.where(first_core, DK, DQ) + i
        return give(
            kind, 0, stage_r.at[i, j, part(r)], r, ret_send_r.at[i, j, r], base_r + j
        )

    far_j = 2 * core
    near_j = 2 * (1 - core)
    flat = 4 * rp

    @pl.when(is_main)
    def _():
        for j in range(2):
            for i in range(2):
                arrive(resident_c + i, base_r + far_j + j)
        for j in range(4):
            for i in range(2):
                block = inbox[resident_c + i, base_r + j]
                plain_r[i, j] = block.astype(jnp.bfloat16)
                stk_r[i, j] = stacked(block)

    def resident_major(both, q):
        at = slice(q * rp, (q + 1) * rp)
        left_c = plain_r[0, :, at].reshape(flat, lane)
        left_d = plain_r[1, :, at].reshape(flat, lane)
        grad_c = grad_d = None
        for r in range(parts):
            for h in range(2):
                a2, b2 = stk_m[0, r, h], stk_m[1, r, h]
                scores = rows_dot(left_c, a2)
                products = rows_dot(left_d, b2)
                term = dot(pgrad_of(scores, products).astype(jnp.bfloat16), a2)
                grad_c = term if grad_c is None else grad_c + term
                if both:
                    term = dot(attn_of(scores).astype(jnp.bfloat16), b2)
                    grad_d = term if grad_d is None else grad_d + term
        stage_r[0, :, at] = grad_c.reshape(4, rp, lane)
        if both:
            stage_r[1, :, at] = grad_d.reshape(4, rp, lane)

    def join_resident(kinds, block, q):
        at = slice(q * rp, (q + 1) * rp)
        for i, kind in enumerate(kinds):
            stage_r[i, near_j + block, at] += stage_o[kind, at]

    def resident_gives(arrays, q):
        return [resident_give(i, far_j + j, q) for j in range(2) for i in arrays] + [
            resident_give(i, near_j + 1 - side, q) for i in arrays
        ]

    for r in range(parts):

        @pl.when(is_main)
        def _(r=r):
            for j in range(4):
                for i in range(2):
                    arrive(mover_a + i, base_m + j, r)
            for j in range(4):
                for i in range(2):
                    block = inbox[mover_a + i, base_m + j, part(r)]
                    low, high = masked(block)
                    at = slice(j * rp, (j + 1) * rp)
                    plain_m[i, r, at] = block.astype(jnp.bfloat16)
                    stk_m[i, r, 0, at] = low
                    stk_m[i, r, 1, at] = high

        def mover_major(both, r):
            grad_a = grad_b = None
            for j in range(4):
                scores = rows_dot(plain_m[0, r], stk_r[0, j])
                products = rows_dot(plain_m[1, r], stk_r[1, j])
                term = dot(pgrad_of(scores, products).astype(jnp.bfloat16), stk_r[0, j])
                grad_a = term if grad_a is None else grad_a + term
                if both:
                    term = dot(attn_of(scores).astype(jnp.bfloat16), stk_r[1, j])
                    grad_b = term if grad_b is None else grad_b + term
            stage_m[0, r] = grad_a
            if both:
                stage_m[1, r] = grad_b

        if r == parts - 1:
            for q in range(parts):
                pl.when(is_main & first_core)(lambda: resident_major(True, q))
                pl.when(is_main & joins_k)(lambda: join_resident((DK, DV), 0, q))
                launch(is_main & first_core, resident_gives((0, 1), q))
            for n in range(parts):
                pl.when(is_main & first_core)(lambda: mover_major(False, n))
                launch(is_main & first_core, [mover_give(0, j, n) for j in range(4)])
        pl.when(is_main & (core == 1))(lambda: mover_major(True, r))
        launch(is_main & (core == 1), [mover_give(i, j, r) for j in range(4) for i in range(2)])

    for q in range(parts):
        pl.when(is_main & (core == 1))(lambda: resident_major(False, q))
        pl.when(is_main & joins_q)(lambda: join_resident((DQ,), 1, q))
        launch(is_main & (core == 1), resident_gives((0,), q))

    @pl.when(is_main & first_core)
    def _():
        totals[DK, :, here] += stage_r[0, near_j + side]
        totals[DV, :, here] += stage_r[1, near_j + side]

    @pl.when(is_main & (core == 1))
    def _():
        totals[DQ, :, here] += stage_r[0, near_j + side]

    @pl.when(outer)
    def _():
        from_line = jnp.where(line == 0, 1, 2)
        for j in range(2):
            for i in range(2):
                arrive(Q - needed + i, 2 * from_line + j)

    def pair_part(w, at_line, j):
        return inbox[w, 2 * at_line + j]

    @pl.when(outer)
    def _():
        k_blocks = [pair_part(K, s_line, j) for j in range(2)]
        v_blocks = [pair_part(V, s_line, j) for j in range(2)]
        k2 = jnp.concatenate([stacked(b) for b in k_blocks], axis=0)
        v2 = jnp.concatenate([stacked(b) for b in v_blocks], axis=0)
        for j in range(2):
            q = pair_part(Q, t_line, j).astype(jnp.bfloat16)
            g = pair_part(G, t_line, j).astype(jnp.bfloat16)
            weight = pgrad_of(rows_dot(q, k2), rows_dot(g, v2))
            stage_a[DQ, j] = dot(weight.astype(jnp.bfloat16), k2)
        q2 = jnp.concatenate([stacked(pair_part(Q, t_line, j)) for j in range(2)], axis=0)
        g2 = jnp.concatenate([stacked(pair_part(G, t_line, j)) for j in range(2)], axis=0)
        for j in range(2):
            scores = rows_dot(k_blocks[j].astype(jnp.bfloat16), q2)
            products = rows_dot(v_blocks[j].astype(jnp.bfloat16), g2)
            stage_a[DK, j] = dot(pgrad_of(scores, products).astype(jnp.bfloat16), q2)
            stage_a[DV, j] = dot(attn_of(scores).astype(jnp.bfloat16), g2)

    @pl.when(outer & joins_k)
    def _():
        for kind in (DK, DV):
            stage_a[kind, 0] += stage_o[kind]

    @pl.when(outer & joins_q)
    def _():
        stage_a[DQ, 1] += stage_o[DQ]

    def pair_give(kind, j, r, target):
        slot = jnp.where(target == other, 1, 0)
        return give(kind, slot, stage_a.at[kind, j, part(r)], r, ret_send_a.at[kind, j, r], target)

    def pair_gives(kinds, j, target):
        return [pair_give(kind, j, r, target) for r in range(parts) for kind in kinds]

    t_here, s_here = line == 3, line == 0
    launch(s_here, [c for j in range(2) for c in pair_gives((DQ,), j, 2 * t_line + j)])
    launch(s_here, pair_gives((DK, DV), 1 - side, other))
    launch(t_here, [c for j in range(2) for c in pair_gives((DK, DV), j, 2 * s_line + j)])
    launch(t_here, pair_gives((DQ,), 1 - side, other))

    @pl.when(t_here)
    def _():
        totals[DQ, :, here] += stage_a[DQ, side]

    @pl.when(s_here)
    def _():
        for kind in (DK, DV):
            totals[kind, :, here] += stage_a[kind, side]

    @pl.when(led)
    def _():
        for i in range(2):
            arrive(2 - lead + i, other)

    late = led | plain
    pl.when(late)(own_pair)

    def own_give(kind, r):
        return give(kind, 2, stage_o.at[kind, part(r)], r, ret_send_o.at[kind, r], other)

    launch(late & (side == 0), [own_give(DQ, r) for r in range(parts)])
    launch(late & (side == 1), [own_give(kind, r) for r in range(parts) for kind in (DK, DV)])

    def taken(kind, slot, p):
        away = side != p
        if slot == 2:
            wanted = side == (1 if kind == DQ else 0)
            other_needed = needed == (Q if kind == DQ else K)
            return away & wanted & (plain | jnp.logical_not(other_needed))
        if kind == DQ:
            if slot == 0:
                return (line > 0) & jnp.where(is_main & (core == 1), away, True)
            return (line == 3) & away
        if slot == 0:
            return (line < 3) & jnp.where(is_main & first_core, away, True)
        return (line == 0) & away

    def take(kind, slot, p, r):
        ref = ret.at[kind, slot, p, part(r)]
        remote(ref, ref, side_send.at[0], ret_recv.at[kind, slot, p, r], other).wait_recv()
        at = slice(r * rp, (r + 1) * rp)
        cols = slice(lane * p, lane * (p + 1))
        totals[kind, at, cols] += ret[kind, slot, p, at]

    def collect(r):
        for slot in (2, 1, 0):
            for kinds in ((DQ,), (DK, DV)):
                for p in range(pairs):

                    @pl.when(taken(kinds[0], slot, p))
                    def _():
                        for kind in kinds:
                            take(kind, slot, p, r)

    def to_head(source, target_ref, n, target):
        return pltpu.make_async_remote_copy(
            src_ref=source,
            dst_ref=target_ref,
            send_sem=reduce_send_sem.at[n],
            recv_sem=reduce_recv_sem.at[n],
            device_id={"head": target},
            device_id_type=MESH,
        )

    def to_core(r, n):
        return to_head(core_send_buf.at[r, n], core_recv_buf.at[r, n], 3 * r + n, core_mate)

    def to_out(r):
        return pltpu.make_async_copy(
            own_part.at[part(r)], own_out.at[part(r)], out_sem.at[r]
        )

    def to_far(r):
        return to_head(far_send_buf.at[r], far_out.at[part(r)], 3 * r + 2, far_mate)

    for r in range(parts):
        collect(r)
        at = slice(r * rp, (r + 1) * rp)
        if r == 0:
            for copy in weight_copies:
                copy.wait()
        final = [totals[i, at].astype(jnp.bfloat16) for i in range(3)]

        def project(target):
            cols = pl.ds(pl.multiple_of(target * out_width, out_width), out_width)
            return sum(dot(final[i], weights[i, :, cols]) for i in range(3))

        core_send_buf[r, 0] = project(2 * (1 - far) + (1 - core))
        to_core(r, 0).start()
        far_send_buf[r] = project(far_mate)
        to_core(r, 0).wait_recv()
        far_send_buf[r] += core_recv_buf[r, 0]
        to_far(r).start()
        core_send_buf[r, 1] = project(core_mate)
        to_core(r, 1).start()
        own_part[at] = project(head)

    for r in range(parts):
        at = slice(r * rp, (r + 1) * rp)
        to_core(r, 1).wait_recv()
        own_part[at] += core_recv_buf[r, 1]
        to_out(r).start()
    for r in range(parts):
        to_far(r).wait_recv()
        to_out(r).wait()

    for r in range(parts):
        to_core(r, 0).wait_send()
        to_core(r, 1).wait_send()
        to_far(r).wait_send()
    for cond, copies in pending:
        if cond is None:
            for copy in copies:
                copy.wait_send()
        else:

            @pl.when(cond)
            def _(copies=copies):
                for copy in copies:
                    copy.wait_send()


def routed_form(n_head, queries, keys, values, out_grad, w_query, w_key, w_value):
    rows, width = queries.shape
    model = w_query.shape[1]
    out_width = model // n_head
    pairs = width // (2 * HD)
    lane = 2 * HD
    blocks = 2 * LINES
    parts = 2
    rp = rows // parts
    f32, bf16 = jnp.float32, jnp.bfloat16
    dma = pltpu.SemaphoreType.DMA
    own_sum, far_sum = pl.pallas_call(
        functools.partial(routed_kernel, parts),
        out_shape=[jax.ShapeDtypeStruct((rows, out_width), f32)] * 2,
        in_specs=[pl.BlockSpec(memory_space=pl.ANY)] * 7,
        out_specs=[pl.BlockSpec(memory_space=pl.ANY)] * 2,
        scratch_shapes=[
            pltpu.VMEM((4, rows, width), bf16),
            pltpu.VMEM((4, pairs, rows, lane), f32),
            pltpu.VMEM((4, blocks, rows, lane), f32),
            pltpu.VMEM((2, 4, rows, lane), bf16),
            pltpu.VMEM((2, 4, 2 * rows, lane), bf16),
            pltpu.VMEM((2, parts, 4 * rp, lane), bf16),
            pltpu.VMEM((2, parts, 2, 4 * rp, lane), bf16),
            pltpu.VMEM((2, parts, 4 * rp, lane), f32),
            pltpu.VMEM((2, 4, rows, lane), f32),
            pltpu.VMEM((3, 2, rows, lane), f32),
            pltpu.VMEM((3, rows, lane), f32),
            pltpu.VMEM((3, 3, pairs, rows, lane), f32),
            pltpu.VMEM((3, width, model), bf16),
            pltpu.VMEM((3, rows, width), f32),
            pltpu.VMEM((rows, out_width), f32),
            pltpu.VMEM((parts, 2, rp, out_width), f32),
            pltpu.VMEM((parts, 2, rp, out_width), f32),
            pltpu.VMEM((parts, rp, out_width), f32),
            dma((4,)),
            dma((3,)),
            dma((parts,)),
            dma((2, pairs, parts)),
            dma((2, pairs)),
            dma((2, pairs)),
            dma((6,)),
            dma((4, blocks, parts)),
            dma((3, 3, pairs, parts)),
            dma((2, 4, parts)),
            dma((2, 4, parts)),
            dma((3, 2, parts)),
            dma((3, parts)),
            dma((3 * parts,)),
            dma((3 * parts,)),
        ],
        compiler_params=pltpu.CompilerParams(collective_id=0, has_side_effects=True),
    )(keys, values, queries, out_grad, w_query, w_key, w_value)
    return (own_sum + far_sum).astype(bf16)


def solution(mesh):
    placed = (
        P("seq", "head"),
        P("seq", "head"),
        P("seq", "head"),
        P("seq", "head"),
        P("head", None),
        P("head", None),
        P("head", None),
    )
    n_seq, n_head = mesh.shape["seq"], mesh.shape["head"]

    def per_device(queries, *rest):
        if n_seq == 2 * LINES and n_head == 4 and queries.shape[1] == 4 * HD:
            return routed_form(n_head, queries, *rest)
        return on_device(queries, *rest)

    return jax.shard_map(
        per_device, mesh=mesh, in_specs=placed, out_specs=P("seq", "head"), check_vma=False
    )
```

```python
import functools

import jax
import jax.numpy as jnp
import numpy as np
from jax import lax
from jax.experimental import pallas as pl
from jax.experimental.pallas import tpu as pltpu
from jax.sharding import PartitionSpec as P

HD = 64
MESH = pl.DeviceIdType.MESH


def shifted(value, axis, steps):
    count = lax.axis_size(axis)
    leading, last = (max(0, -steps), min(count, count - steps))
    return lax.ppermute(value, axis, [(source, source + steps) for source in range(leading, last)])


def pair_tables(width):
    first, second = np.triu_indices(width)
    count = first.shape[0]
    select_first = np.zeros((width, count), np.float32)
    select_second = np.zeros((width, count), np.float32)
    select_first[first, np.arange(count)] = 1.0
    select_second[second, np.arange(count)] = 1.0
    scaling = np.where(first == second, 1.0, np.sqrt(2.0)) / width
    return (select_first, select_second, scaling.astype(np.float32))


def expand_features(inputs, pick_first, pick_second, scaling):
    first = jnp.dot(inputs, pick_first, preferred_element_type=jnp.bfloat16)
    second = jnp.dot(inputs, pick_second, preferred_element_type=jnp.bfloat16)
    feats = (first.astype(jnp.float32) * second.astype(jnp.float32) * scaling).astype(jnp.bfloat16)
    return (first, second, feats)


def chain_back(first, second, dphi, back_first, back_second, scaling):
    scaled = dphi * scaling
    left = scaled * second.astype(jnp.float32)
    right = scaled * first.astype(jnp.float32)
    return jnp.dot(
        left, back_first, precision=lax.Precision.HIGHEST, preferred_element_type=jnp.float32
    ) + jnp.dot(
        right, back_second, precision=lax.Precision.HIGHEST, preferred_element_type=jnp.float32
    )


def on_device(queries, keys, values, out_grad, w_query, w_key, w_value):
    count_rows = queries.shape[0]
    head_count = queries.shape[1] // HD
    select_first, select_second, scale_np = pair_tables(HD)
    pick_first = jnp.asarray(select_first, jnp.bfloat16)
    pick_second = jnp.asarray(select_second, jnp.bfloat16)
    back_first = jnp.asarray(select_first.T, jnp.float32)
    back_second = jnp.asarray(select_second.T, jnp.float32)
    scaling = jnp.asarray(scale_np, jnp.float32)
    feat_count = scale_np.shape[0]
    query_heads = queries.reshape(count_rows, head_count, HD)
    key_heads = keys.reshape(count_rows, head_count, HD)
    value_heads = values.reshape(count_rows, head_count, HD)
    grad_heads = out_grad.reshape(count_rows, head_count, HD)
    query_expanded = []
    key_expanded = []
    kv_parts = []
    grad_parts = []
    for number in range(head_count):
        query_set = expand_features(query_heads[:, number], pick_first, pick_second, scaling)
        key_set = expand_features(key_heads[:, number], pick_first, pick_second, scaling)
        query_expanded.append(query_set)
        key_expanded.append(key_set)
        kv_parts.append(
            jnp.einsum(
                "tf,td->fd", key_set[2], value_heads[:, number], preferred_element_type=jnp.float32
            )
        )
        grad_parts.append(
            jnp.einsum(
                "tf,td->fd", query_set[2], grad_heads[:, number], preferred_element_type=jnp.float32
            )
        )
    kv_local = jnp.stack(kv_parts, 1).reshape(feat_count, head_count * HD)
    grad_local = jnp.stack(grad_parts, 1).reshape(feat_count, head_count * HD)
    rounds = (lax.axis_size("seq") - 1).bit_length()
    kv_running = kv_local
    grad_running = grad_local
    for level in range(rounds):
        kv_running = kv_running + shifted(kv_running, "seq", 1 << level)
        grad_running = grad_running + shifted(grad_running, "seq", -(1 << level))
    kv_before = kv_running - kv_local
    grad_after = grad_running - grad_local
    kv_before = kv_before.astype(jnp.bfloat16).reshape(feat_count, head_count, HD)
    grad_after = grad_after.astype(jnp.bfloat16).reshape(feat_count, head_count, HD)
    causal = lax.broadcasted_iota(jnp.int32, (count_rows, count_rows), 0) >= lax.broadcasted_iota(
        jnp.int32, (count_rows, count_rows), 1
    )
    scores = jnp.einsum("thd,shd->hts", query_heads, key_heads, preferred_element_type=jnp.float32)
    products = jnp.einsum(
        "thd,shd->hts", grad_heads, value_heads, preferred_element_type=jnp.float32
    )
    attn = jnp.where(causal, (scores / HD) ** 2, 0.0).astype(jnp.bfloat16)
    pgrad = jnp.where(causal, 2.0 * scores * products / (HD * HD), 0.0).astype(jnp.bfloat16)
    query_local = jnp.einsum("hts,shd->thd", pgrad, key_heads, preferred_element_type=jnp.float32)
    key_local = jnp.einsum("hts,thd->shd", pgrad, query_heads, preferred_element_type=jnp.float32)
    value_local = jnp.einsum("hts,thd->shd", attn, grad_heads, preferred_element_type=jnp.float32)
    query_out = []
    key_out = []
    value_out = []
    for number in range(head_count):
        qfirst, qsecond, query_feat = query_expanded[number]
        kfirst, ksecond, key_feat = key_expanded[number]
        dfq = jnp.einsum(
            "td,fd->tf",
            grad_heads[:, number],
            kv_before[:, number],
            preferred_element_type=jnp.float32,
        )
        dfk = jnp.einsum(
            "td,fd->tf",
            value_heads[:, number],
            grad_after[:, number],
            preferred_element_type=jnp.float32,
        )
        query_out.append(
            query_local[:, number]
            + chain_back(qfirst, qsecond, dfq, back_first, back_second, scaling)
        )
        key_out.append(
            key_local[:, number]
            + chain_back(kfirst, ksecond, dfk, back_first, back_second, scaling)
        )
        value_out.append(
            value_local[:, number]
            + jnp.einsum(
                "tf,fd->td", key_feat, grad_after[:, number], preferred_element_type=jnp.float32
            )
        )
    query_grad = jnp.stack(query_out, 1).astype(jnp.bfloat16).reshape(count_rows, head_count * HD)
    key_grad = jnp.stack(key_out, 1).astype(jnp.bfloat16).reshape(count_rows, head_count * HD)
    value_grad = jnp.stack(value_out, 1).astype(jnp.bfloat16).reshape(count_rows, head_count * HD)
    partial_sum = jnp.dot(query_grad, w_query, preferred_element_type=jnp.float32)
    partial_sum = partial_sum + jnp.dot(key_grad, w_key, preferred_element_type=jnp.float32)
    partial_sum = partial_sum + jnp.dot(value_grad, w_value, preferred_element_type=jnp.float32)
    return lax.psum_scatter(partial_sum, "head", scatter_dimension=1, tiled=True).astype(
        jnp.bfloat16
    )


def masked(block):
    lanes = lax.broadcasted_iota(jnp.int32, block.shape, 1)
    low = jnp.where(lanes < HD, block, 0.0).astype(jnp.bfloat16)
    high = jnp.where(lanes >= HD, block, 0.0).astype(jnp.bfloat16)
    return low, high


def stacked(block):
    return jnp.concatenate(masked(block), axis=0)


def rows_dot(left, right):
    return lax.dot_general(
        left, right, (((1,), (1,)), ((), ())), preferred_element_type=jnp.float32
    )


def dot(left, right):
    return jnp.dot(left, right, preferred_element_type=jnp.float32)


def pgrad_of(scores, products):
    return scores * products * (2.0 / (HD * HD))


def attn_of(scores):
    scaled = scores * (1.0 / HD)
    return scaled * scaled


K, V, Q, G = range(4)
DQ, DK, DV = range(3)
LINES = 4


def routed_kernel(
    parts,
    k_hbm,
    v_hbm,
    q_hbm,
    g_hbm,
    wq_hbm,
    wk_hbm,
    wv_hbm,
    own_out,
    far_out,
    own,
    mine,
    inbox,
    plain_r,
    stk_r,
    plain_m,
    stk_m,
    stage_m,
    stage_r,
    stage_a,
    stage_o,
    ret,
    weights,
    totals,
    own_part,
    core_send_buf,
    core_recv_buf,
    far_send_buf,
    own_sem,
    weight_sem,
    out_sem,
    mover_send,
    far_send,
    near_send,
    side_send,
    in_recv,
    ret_recv,
    ret_send_m,
    ret_send_r,
    ret_send_a,
    ret_send_o,
    reduce_send_sem,
    reduce_recv_sem,
):
    unused, rows, width = own.shape
    pairs = width // (2 * HD)
    lane = 2 * HD
    rp = rows // parts
    me = lax.axis_index("seq")
    line, side = me // 2, me % 2
    other = 2 * line + (1 - side)
    head = lax.axis_index("head")
    far, core = head // 2, head % 2
    core_mate = 2 * far + (1 - core)
    far_mate = 2 * (1 - far) + core
    out_width = own_out.shape[1]
    first_core = core == 0

    site = 1 + core
    is_main = line == site
    base_m = jnp.where(first_core, 4, 0)
    base_r = 4 - base_m
    is_mover = jnp.where(first_core, line >= 2, line < 2)
    is_far = line == 3 * core
    inner = (line == 1) | (line == 2)
    outer = jnp.logical_not(inner)
    near_target = jnp.where(line == 1, 0, 3)
    t_line = jnp.where(line < 2, 1, 3)
    s_line = t_line - 1
    skips = line % 2 != core
    mover_a = jnp.where(first_core, Q, K)
    resident_c = Q - mover_a
    has_up, has_down = line < LINES - 1, line > 0

    own_copies = [
        pltpu.make_async_copy(source, own.at[i], own_sem.at[i])
        for i, source in enumerate((k_hbm, v_hbm, q_hbm, g_hbm))
    ]
    for copy in own_copies:
        copy.start()

    barrier = pltpu.get_barrier_semaphore()

    def greet(target):
        pl.semaphore_signal(barrier, inc=1, device_id=target, device_id_type=MESH)

    greet({"seq": other})
    greet({"head": core_mate})
    greet({"head": far_mate})
    for cond, there in ((has_up, line + 1), (has_down, line - 1), (skips, 4 - 2 * core - line)):

        @pl.when(cond)
        def _(there=there):
            for p in range(2):
                greet({"seq": 2 * there + p})

    weight_copies = [
        pltpu.make_async_copy(source, weights.at[i], weight_sem.at[i])
        for i, source in enumerate((wq_hbm, wk_hbm, wv_hbm))
    ]
    for copy in weight_copies:
        copy.start()
    for which, copy in enumerate(own_copies):
        copy.wait()
        for p in range(pairs):
            mine[which, p] = own[which, :, lane * p : lane * (p + 1)].astype(jnp.float32)
        inbox[which, me] = mine[which, side]

    pl.semaphore_wait(
        barrier,
        3
        + 2
        * (
            has_up.astype(jnp.int32)
            + has_down.astype(jnp.int32)
            + skips.astype(jnp.int32)
        ),
    )

    def remote(source, target_ref, send, recv, target):
        return pltpu.make_async_remote_copy(
            src_ref=source,
            dst_ref=target_ref,
            send_sem=send,
            recv_sem=recv,
            device_id={"seq": target},
            device_id_type=MESH,
        )

    def part(r):
        return pl.ds(r * rp, rp)

    def mover_copy(i, p, r):
        w = mover_a + i
        return remote(
            mine.at[w, p, part(r)],
            inbox.at[w, me, part(r)],
            mover_send.at[i, p, r],
            in_recv.at[w, me, r],
            2 * site + p,
        )

    def whole_copy(w, p, send, target):
        return remote(mine.at[w, p], inbox.at[w, me], send, in_recv.at[w, me, 0], target)

    def far_copy(i, p):
        return whole_copy(resident_c + i, p, far_send.at[i, p], 2 * site + p)

    def near_copy(i, p):
        return whole_copy(near_a + i, p, near_send.at[i, p], 2 * near_target + p)

    lead = 2 * side
    near_a = jnp.where(line % 2 == 1, Q, K)
    needed = jnp.where(outer, 2 * (line // 2), resident_c)
    plain = inner & jnp.logical_not(is_main)
    sent = jnp.where(plain, lead, needed)
    got = jnp.where(plain, 2 - lead, needed)
    leads, led = sent != lead, got != 2 - lead

    def exchange_copy(i):
        return whole_copy(sent + i, 1 - side, side_send.at[i], other)

    def lead_copy(i):
        return whole_copy(lead + i, 1 - side, side_send.at[4 + i], other)

    pending = []

    def launch(cond, copies, again=False):
        if not again:
            pending.append((cond, copies))
        if cond is None:
            for copy in copies:
                copy.start()
        else:

            @pl.when(cond)
            def _():
                for copy in copies:
                    copy.start()

    crossing = [(i, p) for p in range(pairs) for i in range(2)]
    movers_of = [[mover_copy(i, p, r) for i, p in crossing] for r in range(parts)]
    far_copies = [far_copy(i, p) for i, p in crossing]
    near_copies = [near_copy(i, p) for i, p in crossing]
    exchanges = [exchange_copy(i) for i in range(2)]
    lead_copies = [lead_copy(i) for i in range(2)]

    launch(is_mover, movers_of[0])
    launch(is_far, far_copies)
    launch(jnp.logical_not(plain), exchanges)
    launch(inner, near_copies)
    for r in range(1, parts):
        launch(is_mover, movers_of[r])
    launch(plain, exchanges)
    launch(leads, lead_copies)

    def arrive(w, b, r=None):
        ref = inbox.at[w, b] if r is None else inbox.at[w, b, part(r)]
        sem = in_recv.at[w, b, 0 if r is None else r]
        remote(ref, ref, side_send.at[0], sem, other).wait_recv()

    def columns(p):
        return pl.ds(pl.multiple_of(p * lane, lane), lane)

    def diagonal(p):
        cols = columns(p)
        t = lax.broadcasted_iota(jnp.int32, (rows, 2 * rows), 0)
        s = lax.broadcasted_iota(jnp.int32, (rows, 2 * rows), 1) % rows
        k2, v2 = stacked(mine[K, p]), stacked(mine[V, p])
        weight = pgrad_of(rows_dot(own[Q, :, cols], k2), rows_dot(own[G, :, cols], v2))
        weight = jnp.where(t >= s, weight, 0.0)
        totals[DQ, :, cols] = dot(weight.astype(jnp.bfloat16), k2)
        q2, g2 = stacked(mine[Q, p]), stacked(mine[G, p])
        scores = rows_dot(own[K, :, cols], q2)
        weight = pgrad_of(scores, rows_dot(own[V, :, cols], g2))
        weight = jnp.where(s >= t, weight, 0.0)
        attn = jnp.where(s >= t, attn_of(scores), 0.0)
        totals[DK, :, cols] = dot(weight.astype(jnp.bfloat16), q2)
        totals[DV, :, cols] = dot(attn.astype(jnp.bfloat16), g2)

    for p in range(pairs):
        diagonal(p)

    for i in range(2):
        arrive(got + i, other)

    def give(kind, slot, source, r, send, target):
        return remote(
            source, ret.at[kind, slot, side, part(r)], send, ret_recv.at[kind, slot, side, r], target
        )

    here = columns(side)

    def own_pair():
        even, odd = 2 * line, 2 * line + 1
        k, v, q, g = inbox[K, even], inbox[V, even], inbox[Q, odd], inbox[G, odd]
        k2, v2 = stacked(k), stacked(v)
        weight = pgrad_of(
            rows_dot(q.astype(jnp.bfloat16), k2), rows_dot(g.astype(jnp.bfloat16), v2)
        )
        stage_o[DQ] = dot(weight.astype(jnp.bfloat16), k2)
        q2, g2 = stacked(q), stacked(g)
        scores = rows_dot(k.astype(jnp.bfloat16), q2)
        weight = pgrad_of(scores, rows_dot(v.astype(jnp.bfloat16), g2))
        stage_o[DK] = dot(weight.astype(jnp.bfloat16), q2)
        stage_o[DV] = dot(attn_of(scores).astype(jnp.bfloat16), g2)

        @pl.when(side == 1)
        def _():
            totals[DQ, :, here] += stage_o[DQ]

        @pl.when(side == 0)
        def _():
            for kind in (DK, DV):
                totals[kind, :, here] += stage_o[kind]

    early = jnp.logical_not(led | plain)
    joins_k, joins_q = early & (side == 1), early & (side == 0)
    pl.when(early)(own_pair)
    every = [(j, r) for r in range(parts) for j in range(2)]

    def mover_give(i, j, r):
        kind = jnp.where(first_core, DQ, DK) + i
        return give(
            kind,
            0,
            stage_m.at[i, r, pl.ds(j * rp, rp)],
            r,
            ret_send_m.at[i, j, r],
            base_m + j,
        )

    def resident_give(i, j, r):
        kind = jnp.where(first_core, DK, DQ) + i
        return give(
            kind, 0, stage_r.at[i, j, part(r)], r, ret_send_r.at[i, j, r], base_r + j
        )

    far_j = 2 * core
    near_j = 2 * (1 - core)
    flat = 4 * rp

    @pl.when(is_main)
    def _():
        for j in range(2):
            for i in range(2):
                arrive(resident_c + i, base_r + far_j + j)
        for j in range(4):
            for i in range(2):
                block = inbox[resident_c + i, base_r + j]
                plain_r[i, j] = block.astype(jnp.bfloat16)
                stk_r[i, j] = stacked(block)

    def resident_major(both, q):
        at = slice(q * rp, (q + 1) * rp)
        left_c = plain_r[0, :, at].reshape(flat, lane)
        left_d = plain_r[1, :, at].reshape(flat, lane)
        grad_c = grad_d = None
        for r in range(parts):
            for h in range(2):
                a2, b2 = stk_m[0, r, h], stk_m[1, r, h]
                scores = rows_dot(left_c, a2)
                products = rows_dot(left_d, b2)
                term = dot(pgrad_of(scores, products).astype(jnp.bfloat16), a2)
                grad_c = term if grad_c is None else grad_c + term
                if both:
                    term = dot(attn_of(scores).astype(jnp.bfloat16), b2)
                    grad_d = term if grad_d is None else grad_d + term
        stage_r[0, :, at] = grad_c.reshape(4, rp, lane)
        if both:
            stage_r[1, :, at] = grad_d.reshape(4, rp, lane)

    def join_resident(kinds, block, q):
        at = slice(q * rp, (q + 1) * rp)
        for i, kind in enumerate(kinds):
            stage_r[i, near_j + block, at] += stage_o[kind, at]

    def resident_gives(arrays, q):
        return [resident_give(i, far_j + j, q) for j in range(2) for i in arrays] + [
            resident_give(i, near_j + 1 - side, q) for i in arrays
        ]

    for r in range(parts):

        @pl.when(is_main)
        def _(r=r):
            for j in range(4):
                for i in range(2):
                    arrive(mover_a + i, base_m + j, r)
            for j in range(4):
                for i in range(2):
                    block = inbox[mover_a + i, base_m + j, part(r)]
                    low, high = masked(block)
                    at = slice(j * rp, (j + 1) * rp)
                    plain_m[i, r, at] = block.astype(jnp.bfloat16)
                    stk_m[i, r, 0, at] = low
                    stk_m[i, r, 1, at] = high

        def mover_major(both, r):
            grad_a = grad_b = None
            for j in range(4):
                scores = rows_dot(plain_m[0, r], stk_r[0, j])
                products = rows_dot(plain_m[1, r], stk_r[1, j])
                term = dot(pgrad_of(scores, products).astype(jnp.bfloat16), stk_r[0, j])
                grad_a = term if grad_a is None else grad_a + term
                if both:
                    term = dot(attn_of(scores).astype(jnp.bfloat16), stk_r[1, j])
                    grad_b = term if grad_b is None else grad_b + term
            stage_m[0, r] = grad_a
            if both:
                stage_m[1, r] = grad_b

        if r == parts - 1:
            for q in range(parts):
                pl.when(is_main & first_core)(lambda: resident_major(True, q))
                pl.when(is_main & joins_k)(lambda: join_resident((DK, DV), 0, q))
                launch(is_main & first_core, resident_gives((0, 1), q))
            for n in range(parts):
                pl.when(is_main & first_core)(lambda: mover_major(False, n))
                launch(is_main & first_core, [mover_give(0, j, n) for j in range(4)])
        pl.when(is_main & (core == 1))(lambda: mover_major(True, r))
        launch(is_main & (core == 1), [mover_give(i, j, r) for j in range(4) for i in range(2)])

    for q in range(parts):
        pl.when(is_main & (core == 1))(lambda: resident_major(False, q))
        pl.when(is_main & joins_q)(lambda: join_resident((DQ,), 1, q))
        launch(is_main & (core == 1), resident_gives((0,), q))

    @pl.when(is_main & first_core)
    def _():
        totals[DK, :, here] += stage_r[0, near_j + side]
        totals[DV, :, here] += stage_r[1, near_j + side]

    @pl.when(is_main & (core == 1))
    def _():
        totals[DQ, :, here] += stage_r[0, near_j + side]

    @pl.when(outer)
    def _():
        from_line = jnp.where(line == 0, 1, 2)
        for j in range(2):
            for i in range(2):
                arrive(Q - needed + i, 2 * from_line + j)

    def pair_part(w, at_line, j):
        return inbox[w, 2 * at_line + j]

    @pl.when(outer)
    def _():
        k_blocks = [pair_part(K, s_line, j) for j in range(2)]
        v_blocks = [pair_part(V, s_line, j) for j in range(2)]
        k2 = jnp.concatenate([stacked(b) for b in k_blocks], axis=0)
        v2 = jnp.concatenate([stacked(b) for b in v_blocks], axis=0)
        for j in range(2):
            q = pair_part(Q, t_line, j).astype(jnp.bfloat16)
            g = pair_part(G, t_line, j).astype(jnp.bfloat16)
            weight = pgrad_of(rows_dot(q, k2), rows_dot(g, v2))
            stage_a[DQ, j] = dot(weight.astype(jnp.bfloat16), k2)
        q2 = jnp.concatenate([stacked(pair_part(Q, t_line, j)) for j in range(2)], axis=0)
        g2 = jnp.concatenate([stacked(pair_part(G, t_line, j)) for j in range(2)], axis=0)
        for j in range(2):
            scores = rows_dot(k_blocks[j].astype(jnp.bfloat16), q2)
            products = rows_dot(v_blocks[j].astype(jnp.bfloat16), g2)
            stage_a[DK, j] = dot(pgrad_of(scores, products).astype(jnp.bfloat16), q2)
            stage_a[DV, j] = dot(attn_of(scores).astype(jnp.bfloat16), g2)

    @pl.when(outer & joins_k)
    def _():
        for kind in (DK, DV):
            stage_a[kind, 0] += stage_o[kind]

    @pl.when(outer & joins_q)
    def _():
        stage_a[DQ, 1] += stage_o[DQ]

    def pair_give(kind, j, r, target):
        slot = jnp.where(target == other, 1, 0)
        return give(kind, slot, stage_a.at[kind, j, part(r)], r, ret_send_a.at[kind, j, r], target)

    def pair_gives(kinds, j, target):
        return [pair_give(kind, j, r, target) for r in range(parts) for kind in kinds]

    t_here, s_here = line == 3, line == 0
    launch(s_here, [c for j in range(2) for c in pair_gives((DQ,), j, 2 * t_line + j)])
    launch(s_here, pair_gives((DK, DV), 1 - side, other))
    launch(t_here, [c for j in range(2) for c in pair_gives((DK, DV), j, 2 * s_line + j)])
    launch(t_here, pair_gives((DQ,), 1 - side, other))

    @pl.when(t_here)
    def _():
        totals[DQ, :, here] += stage_a[DQ, side]

    @pl.when(s_here)
    def _():
        for kind in (DK, DV):
            totals[kind, :, here] += stage_a[kind, side]

    @pl.when(led)
    def _():
        for i in range(2):
            arrive(2 - lead + i, other)

    late = led | plain
    pl.when(late)(own_pair)

    def own_give(kind, r):
        return give(kind, 2, stage_o.at[kind, part(r)], r, ret_send_o.at[kind, r], other)

    launch(late & (side == 0), [own_give(DQ, r) for r in range(parts)])
    launch(late & (side == 1), [own_give(kind, r) for r in range(parts) for kind in (DK, DV)])

    def taken(kind, slot, p):
        away = side != p
        if slot == 2:
            wanted = side == (1 if kind == DQ else 0)
            other_needed = needed == (Q if kind == DQ else K)
            return away & wanted & (plain | jnp.logical_not(other_needed))
        if kind == DQ:
            if slot == 0:
                return (line > 0) & jnp.where(is_main & (core == 1), away, True)
            return (line == 3) & away
        if slot == 0:
            return (line < 3) & jnp.where(is_main & first_core, away, True)
        return (line == 0) & away

    def take(kind, slot, p, r):
        ref = ret.at[kind, slot, p, part(r)]
        remote(ref, ref, side_send.at[0], ret_recv.at[kind, slot, p, r], other).wait_recv()
        at = slice(r * rp, (r + 1) * rp)
        cols = slice(lane * p, lane * (p + 1))
        totals[kind, at, cols] += ret[kind, slot, p, at]

    def collect(r):
        for slot in (2, 1, 0):
            for kinds in ((DQ,), (DK, DV)):
                for p in range(pairs):

                    @pl.when(taken(kinds[0], slot, p))
                    def _():
                        for kind in kinds:
                            take(kind, slot, p, r)

    def to_head(source, target_ref, n, target):
        return pltpu.make_async_remote_copy(
            src_ref=source,
            dst_ref=target_ref,
            send_sem=reduce_send_sem.at[n],
            recv_sem=reduce_recv_sem.at[n],
            device_id={"head": target},
            device_id_type=MESH,
        )

    def to_core(r, n):
        return to_head(core_send_buf.at[r, n], core_recv_buf.at[r, n], 3 * r + n, core_mate)

    def to_out(r):
        return pltpu.make_async_copy(
            own_part.at[part(r)], own_out.at[part(r)], out_sem.at[r]
        )

    def to_far(r):
        return to_head(far_send_buf.at[r], far_out.at[part(r)], 3 * r + 2, far_mate)

    for r in range(parts):
        collect(r)
        at = slice(r * rp, (r + 1) * rp)
        if r == 0:
            for copy in weight_copies:
                copy.wait()
        final = [totals[i, at].astype(jnp.bfloat16) for i in range(3)]

        def project(target):
            cols = pl.ds(pl.multiple_of(target * out_width, out_width), out_width)
            return sum(dot(final[i], weights[i, :, cols]) for i in range(3))

        core_send_buf[r, 0] = project(2 * (1 - far) + (1 - core))
        to_core(r, 0).start()
        far_send_buf[r] = project(far_mate)
        core_send_buf[r, 1] = project(core_mate)
        to_core(r, 1).start()
        to_core(r, 0).wait_recv()
        far_send_buf[r] += core_recv_buf[r, 0]
        to_far(r).start()
        own_part[at] = project(head)

    for r in range(parts):
        at = slice(r * rp, (r + 1) * rp)
        to_core(r, 1).wait_recv()
        own_part[at] += core_recv_buf[r, 1]
        to_out(r).start()
    for r in range(parts):
        to_far(r).wait_recv()
        to_out(r).wait()

    for r in range(parts):
        to_core(r, 0).wait_send()
        to_core(r, 1).wait_send()
        to_far(r).wait_send()
    for cond, copies in pending:
        if cond is None:
            for copy in copies:
                copy.wait_send()
        else:

            @pl.when(cond)
            def _(copies=copies):
                for copy in copies:
                    copy.wait_send()


def routed_form(n_head, queries, keys, values, out_grad, w_query, w_key, w_value):
    rows, width = queries.shape
    model = w_query.shape[1]
    out_width = model // n_head
    pairs = width // (2 * HD)
    lane = 2 * HD
    blocks = 2 * LINES
    parts = 2
    rp = rows // parts
    f32, bf16 = jnp.float32, jnp.bfloat16
    dma = pltpu.SemaphoreType.DMA
    own_sum, far_sum = pl.pallas_call(
        functools.partial(routed_kernel, parts),
        out_shape=[jax.ShapeDtypeStruct((rows, out_width), f32)] * 2,
        in_specs=[pl.BlockSpec(memory_space=pl.ANY)] * 7,
        out_specs=[pl.BlockSpec(memory_space=pl.ANY)] * 2,
        scratch_shapes=[
            pltpu.VMEM((4, rows, width), bf16),
            pltpu.VMEM((4, pairs, rows, lane), f32),
            pltpu.VMEM((4, blocks, rows, lane), f32),
            pltpu.VMEM((2, 4, rows, lane), bf16),
            pltpu.VMEM((2, 4, 2 * rows, lane), bf16),
            pltpu.VMEM((2, parts, 4 * rp, lane), bf16),
            pltpu.VMEM((2, parts, 2, 4 * rp, lane), bf16),
            pltpu.VMEM((2, parts, 4 * rp, lane), f32),
            pltpu.VMEM((2, 4, rows, lane), f32),
            pltpu.VMEM((3, 2, rows, lane), f32),
            pltpu.VMEM((3, rows, lane), f32),
            pltpu.VMEM((3, 3, pairs, rows, lane), f32),
            pltpu.VMEM((3, width, model), bf16),
            pltpu.VMEM((3, rows, width), f32),
            pltpu.VMEM((rows, out_width), f32),
            pltpu.VMEM((parts, 2, rp, out_width), f32),
            pltpu.VMEM((parts, 2, rp, out_width), f32),
            pltpu.VMEM((parts, rp, out_width), f32),
            dma((4,)),
            dma((3,)),
            dma((parts,)),
            dma((2, pairs, parts)),
            dma((2, pairs)),
            dma((2, pairs)),
            dma((6,)),
            dma((4, blocks, parts)),
            dma((3, 3, pairs, parts)),
            dma((2, 4, parts)),
            dma((2, 4, parts)),
            dma((3, 2, parts)),
            dma((3, parts)),
            dma((3 * parts,)),
            dma((3 * parts,)),
        ],
        compiler_params=pltpu.CompilerParams(collective_id=0, has_side_effects=True),
    )(keys, values, queries, out_grad, w_query, w_key, w_value)
    return (own_sum + far_sum).astype(bf16)


def solution(mesh):
    placed = (
        P("seq", "head"),
        P("seq", "head"),
        P("seq", "head"),
        P("seq", "head"),
        P("head", None),
        P("head", None),
        P("head", None),
    )
    n_seq, n_head = mesh.shape["seq"], mesh.shape["head"]

    def per_device(queries, *rest):
        if n_seq == 2 * LINES and n_head == 4 and queries.shape[1] == 4 * HD:
            return routed_form(n_head, queries, *rest)
        return on_device(queries, *rest)

    return jax.shard_map(
        per_device, mesh=mesh, in_specs=placed, out_specs=P("seq", "head"), check_vma=False
    )
```

```python
import functools

import jax
import jax.numpy as jnp
import numpy as np
from jax import lax
from jax.experimental import pallas as pl
from jax.experimental.pallas import tpu as pltpu
from jax.sharding import PartitionSpec as P

HD = 64
MESH = pl.DeviceIdType.MESH


def shifted(value, axis, steps):
    count = lax.axis_size(axis)
    leading, last = (max(0, -steps), min(count, count - steps))
    return lax.ppermute(value, axis, [(source, source + steps) for source in range(leading, last)])


def pair_tables(width):
    first, second = np.triu_indices(width)
    count = first.shape[0]
    select_first = np.zeros((width, count), np.float32)
    select_second = np.zeros((width, count), np.float32)
    select_first[first, np.arange(count)] = 1.0
    select_second[second, np.arange(count)] = 1.0
    scaling = np.where(first == second, 1.0, np.sqrt(2.0)) / width
    return (select_first, select_second, scaling.astype(np.float32))


def expand_features(inputs, pick_first, pick_second, scaling):
    first = jnp.dot(inputs, pick_first, preferred_element_type=jnp.bfloat16)
    second = jnp.dot(inputs, pick_second, preferred_element_type=jnp.bfloat16)
    feats = (first.astype(jnp.float32) * second.astype(jnp.float32) * scaling).astype(jnp.bfloat16)
    return (first, second, feats)


def chain_back(first, second, dphi, back_first, back_second, scaling):
    scaled = dphi * scaling
    left = scaled * second.astype(jnp.float32)
    right = scaled * first.astype(jnp.float32)
    return jnp.dot(
        left, back_first, precision=lax.Precision.HIGHEST, preferred_element_type=jnp.float32
    ) + jnp.dot(
        right, back_second, precision=lax.Precision.HIGHEST, preferred_element_type=jnp.float32
    )


def on_device(queries, keys, values, out_grad, w_query, w_key, w_value):
    count_rows = queries.shape[0]
    head_count = queries.shape[1] // HD
    select_first, select_second, scale_np = pair_tables(HD)
    pick_first = jnp.asarray(select_first, jnp.bfloat16)
    pick_second = jnp.asarray(select_second, jnp.bfloat16)
    back_first = jnp.asarray(select_first.T, jnp.float32)
    back_second = jnp.asarray(select_second.T, jnp.float32)
    scaling = jnp.asarray(scale_np, jnp.float32)
    feat_count = scale_np.shape[0]
    query_heads = queries.reshape(count_rows, head_count, HD)
    key_heads = keys.reshape(count_rows, head_count, HD)
    value_heads = values.reshape(count_rows, head_count, HD)
    grad_heads = out_grad.reshape(count_rows, head_count, HD)
    query_expanded = []
    key_expanded = []
    kv_parts = []
    grad_parts = []
    for number in range(head_count):
        query_set = expand_features(query_heads[:, number], pick_first, pick_second, scaling)
        key_set = expand_features(key_heads[:, number], pick_first, pick_second, scaling)
        query_expanded.append(query_set)
        key_expanded.append(key_set)
        kv_parts.append(
            jnp.einsum(
                "tf,td->fd", key_set[2], value_heads[:, number], preferred_element_type=jnp.float32
            )
        )
        grad_parts.append(
            jnp.einsum(
                "tf,td->fd", query_set[2], grad_heads[:, number], preferred_element_type=jnp.float32
            )
        )
    kv_local = jnp.stack(kv_parts, 1).reshape(feat_count, head_count * HD)
    grad_local = jnp.stack(grad_parts, 1).reshape(feat_count, head_count * HD)
    rounds = (lax.axis_size("seq") - 1).bit_length()
    kv_running = kv_local
    grad_running = grad_local
    for level in range(rounds):
        kv_running = kv_running + shifted(kv_running, "seq", 1 << level)
        grad_running = grad_running + shifted(grad_running, "seq", -(1 << level))
    kv_before = kv_running - kv_local
    grad_after = grad_running - grad_local
    kv_before = kv_before.astype(jnp.bfloat16).reshape(feat_count, head_count, HD)
    grad_after = grad_after.astype(jnp.bfloat16).reshape(feat_count, head_count, HD)
    causal = lax.broadcasted_iota(jnp.int32, (count_rows, count_rows), 0) >= lax.broadcasted_iota(
        jnp.int32, (count_rows, count_rows), 1
    )
    scores = jnp.einsum("thd,shd->hts", query_heads, key_heads, preferred_element_type=jnp.float32)
    products = jnp.einsum(
        "thd,shd->hts", grad_heads, value_heads, preferred_element_type=jnp.float32
    )
    attn = jnp.where(causal, (scores / HD) ** 2, 0.0).astype(jnp.bfloat16)
    pgrad = jnp.where(causal, 2.0 * scores * products / (HD * HD), 0.0).astype(jnp.bfloat16)
    query_local = jnp.einsum("hts,shd->thd", pgrad, key_heads, preferred_element_type=jnp.float32)
    key_local = jnp.einsum("hts,thd->shd", pgrad, query_heads, preferred_element_type=jnp.float32)
    value_local = jnp.einsum("hts,thd->shd", attn, grad_heads, preferred_element_type=jnp.float32)
    query_out = []
    key_out = []
    value_out = []
    for number in range(head_count):
        qfirst, qsecond, query_feat = query_expanded[number]
        kfirst, ksecond, key_feat = key_expanded[number]
        dfq = jnp.einsum(
            "td,fd->tf",
            grad_heads[:, number],
            kv_before[:, number],
            preferred_element_type=jnp.float32,
        )
        dfk = jnp.einsum(
            "td,fd->tf",
            value_heads[:, number],
            grad_after[:, number],
            preferred_element_type=jnp.float32,
        )
        query_out.append(
            query_local[:, number]
            + chain_back(qfirst, qsecond, dfq, back_first, back_second, scaling)
        )
        key_out.append(
            key_local[:, number]
            + chain_back(kfirst, ksecond, dfk, back_first, back_second, scaling)
        )
        value_out.append(
            value_local[:, number]
            + jnp.einsum(
                "tf,fd->td", key_feat, grad_after[:, number], preferred_element_type=jnp.float32
            )
        )
    query_grad = jnp.stack(query_out, 1).astype(jnp.bfloat16).reshape(count_rows, head_count * HD)
    key_grad = jnp.stack(key_out, 1).astype(jnp.bfloat16).reshape(count_rows, head_count * HD)
    value_grad = jnp.stack(value_out, 1).astype(jnp.bfloat16).reshape(count_rows, head_count * HD)
    partial_sum = jnp.dot(query_grad, w_query, preferred_element_type=jnp.float32)
    partial_sum = partial_sum + jnp.dot(key_grad, w_key, preferred_element_type=jnp.float32)
    partial_sum = partial_sum + jnp.dot(value_grad, w_value, preferred_element_type=jnp.float32)
    return lax.psum_scatter(partial_sum, "head", scatter_dimension=1, tiled=True).astype(
        jnp.bfloat16
    )


def masked(block):
    lanes = lax.broadcasted_iota(jnp.int32, block.shape, 1)
    low = jnp.where(lanes < HD, block, 0.0).astype(jnp.bfloat16)
    high = jnp.where(lanes >= HD, block, 0.0).astype(jnp.bfloat16)
    return low, high


def stacked(block):
    return jnp.concatenate(masked(block), axis=0)


def rows_dot(left, right):
    return lax.dot_general(
        left, right, (((1,), (1,)), ((), ())), preferred_element_type=jnp.float32
    )


def dot(left, right):
    return jnp.dot(left, right, preferred_element_type=jnp.float32)


def pgrad_of(scores, products):
    return scores * products * (2.0 / (HD * HD))


def attn_of(scores):
    scaled = scores * (1.0 / HD)
    return scaled * scaled


K, V, Q, G = range(4)
DQ, DK, DV = range(3)
LINES = 4


def routed_kernel(
    parts,
    k_hbm,
    v_hbm,
    q_hbm,
    g_hbm,
    wq_hbm,
    wk_hbm,
    wv_hbm,
    own_out,
    far_out,
    own,
    mine,
    inbox,
    plain_r,
    stk_r,
    plain_m,
    stk_m,
    stage_m,
    stage_r,
    stage_a,
    stage_o,
    ret,
    weights,
    totals,
    own_part,
    core_send_buf,
    core_recv_buf,
    far_send_buf,
    own_sem,
    weight_sem,
    out_sem,
    mover_send,
    far_send,
    near_send,
    side_send,
    in_recv,
    ret_recv,
    ret_send_m,
    ret_send_r,
    ret_send_a,
    ret_send_o,
    reduce_send_sem,
    reduce_recv_sem,
):
    unused, rows, width = own.shape
    pairs = width // (2 * HD)
    lane = 2 * HD
    rp = rows // parts
    me = lax.axis_index("seq")
    line, side = me // 2, me % 2
    other = 2 * line + (1 - side)
    head = lax.axis_index("head")
    far, core = head // 2, head % 2
    core_mate = 2 * far + (1 - core)
    far_mate = 2 * (1 - far) + core
    out_width = own_out.shape[1]
    first_core = core == 0

    site = 1 + core
    is_main = line == site
    base_m = jnp.where(first_core, 4, 0)
    base_r = 4 - base_m
    is_mover = jnp.where(first_core, line >= 2, line < 2)
    is_far = line == 3 * core
    inner = (line == 1) | (line == 2)
    outer = jnp.logical_not(inner)
    near_target = jnp.where(line == 1, 0, 3)
    t_line = jnp.where(line < 2, 1, 3)
    s_line = t_line - 1
    skips = line % 2 != core
    mover_a = jnp.where(first_core, Q, K)
    resident_c = Q - mover_a
    has_up, has_down = line < LINES - 1, line > 0

    own_copies = [
        pltpu.make_async_copy(source, own.at[i], own_sem.at[i])
        for i, source in enumerate((k_hbm, v_hbm, q_hbm, g_hbm))
    ]
    for copy in own_copies:
        copy.start()

    barrier = pltpu.get_barrier_semaphore()

    def greet(target):
        pl.semaphore_signal(barrier, inc=1, device_id=target, device_id_type=MESH)

    greet({"seq": other})
    greet({"head": core_mate})
    greet({"head": far_mate})
    for cond, there in ((has_up, line + 1), (has_down, line - 1), (skips, 4 - 2 * core - line)):

        @pl.when(cond)
        def _(there=there):
            for p in range(2):
                greet({"seq": 2 * there + p})

    weight_copies = [
        pltpu.make_async_copy(source, weights.at[i], weight_sem.at[i])
        for i, source in enumerate((wq_hbm, wk_hbm, wv_hbm))
    ]
    for copy in weight_copies:
        copy.start()
    for which, copy in enumerate(own_copies):
        copy.wait()
        for p in range(pairs):
            mine[which, p] = own[which, :, lane * p : lane * (p + 1)].astype(jnp.float32)
        inbox[which, me] = mine[which, side]

    pl.semaphore_wait(
        barrier,
        3
        + 2
        * (
            has_up.astype(jnp.int32)
            + has_down.astype(jnp.int32)
            + skips.astype(jnp.int32)
        ),
    )

    def remote(source, target_ref, send, recv, target):
        return pltpu.make_async_remote_copy(
            src_ref=source,
            dst_ref=target_ref,
            send_sem=send,
            recv_sem=recv,
            device_id={"seq": target},
            device_id_type=MESH,
        )

    def part(r):
        return pl.ds(r * rp, rp)

    def mover_copy(i, p, r):
        w = mover_a + i
        return remote(
            mine.at[w, p, part(r)],
            inbox.at[w, me, part(r)],
            mover_send.at[i, p, r],
            in_recv.at[w, me, r],
            2 * site + p,
        )

    def whole_copy(w, p, send, target):
        return remote(mine.at[w, p], inbox.at[w, me], send, in_recv.at[w, me, 0], target)

    def far_copy(i, p):
        return whole_copy(resident_c + i, p, far_send.at[i, p], 2 * site + p)

    def near_copy(i, p):
        return whole_copy(near_a + i, p, near_send.at[i, p], 2 * near_target + p)

    lead = 2 * side
    near_a = jnp.where(line % 2 == 1, Q, K)
    needed = jnp.where(outer, 2 * (line // 2), resident_c)
    plain = inner & jnp.logical_not(is_main)
    sent = jnp.where(plain, lead, needed)
    got = jnp.where(plain, 2 - lead, needed)
    leads, led = sent != lead, got != 2 - lead

    def exchange_copy(i):
        return whole_copy(sent + i, 1 - side, side_send.at[i], other)

    def lead_copy(i):
        return whole_copy(lead + i, 1 - side, side_send.at[4 + i], other)

    pending = []

    def launch(cond, copies, again=False):
        if not again:
            pending.append((cond, copies))
        if cond is None:
            for copy in copies:
                copy.start()
        else:

            @pl.when(cond)
            def _():
                for copy in copies:
                    copy.start()

    crossing = [(i, p) for p in range(pairs) for i in range(2)]
    movers_of = [[mover_copy(i, p, r) for i, p in crossing] for r in range(parts)]
    far_copies = [far_copy(i, p) for i, p in crossing]
    near_copies = [near_copy(i, p) for i, p in crossing]
    exchanges = [exchange_copy(i) for i in range(2)]
    lead_copies = [lead_copy(i) for i in range(2)]

    launch(is_mover, movers_of[0])
    launch(is_far, far_copies)
    launch(jnp.logical_not(plain), exchanges)
    launch(inner, near_copies)
    for r in range(1, parts):
        launch(is_mover, movers_of[r])
    launch(plain, exchanges)
    launch(leads, lead_copies)

    def arrive(w, b, r=None):
        ref = inbox.at[w, b] if r is None else inbox.at[w, b, part(r)]
        sem = in_recv.at[w, b, 0 if r is None else r]
        remote(ref, ref, side_send.at[0], sem, other).wait_recv()

    def columns(p):
        return pl.ds(pl.multiple_of(p * lane, lane), lane)

    def diagonal(p):
        cols = columns(p)
        t = lax.broadcasted_iota(jnp.int32, (rows, 2 * rows), 0)
        s = lax.broadcasted_iota(jnp.int32, (rows, 2 * rows), 1) % rows
        k2, v2 = stacked(mine[K, p]), stacked(mine[V, p])
        weight = pgrad_of(rows_dot(own[Q, :, cols], k2), rows_dot(own[G, :, cols], v2))
        weight = jnp.where(t >= s, weight, 0.0)
        totals[DQ, :, cols] = dot(weight.astype(jnp.bfloat16), k2)
        q2, g2 = stacked(mine[Q, p]), stacked(mine[G, p])
        scores = rows_dot(own[K, :, cols], q2)
        weight = pgrad_of(scores, rows_dot(own[V, :, cols], g2))
        weight = jnp.where(s >= t, weight, 0.0)
        attn = jnp.where(s >= t, attn_of(scores), 0.0)
        totals[DK, :, cols] = dot(weight.astype(jnp.bfloat16), q2)
        totals[DV, :, cols] = dot(attn.astype(jnp.bfloat16), g2)

    for p in range(pairs):
        diagonal(p)

    for i in range(2):
        arrive(got + i, other)

    def give(kind, slot, source, r, send, target):
        return remote(
            source, ret.at[kind, slot, side, part(r)], send, ret_recv.at[kind, slot, side, r], target
        )

    here = columns(side)

    def own_pair():
        even, odd = 2 * line, 2 * line + 1
        k, v, q, g = inbox[K, even], inbox[V, even], inbox[Q, odd], inbox[G, odd]
        k2, v2 = stacked(k), stacked(v)
        weight = pgrad_of(
            rows_dot(q.astype(jnp.bfloat16), k2), rows_dot(g.astype(jnp.bfloat16), v2)
        )
        stage_o[DQ] = dot(weight.astype(jnp.bfloat16), k2)
        q2, g2 = stacked(q), stacked(g)
        scores = rows_dot(k.astype(jnp.bfloat16), q2)
        weight = pgrad_of(scores, rows_dot(v.astype(jnp.bfloat16), g2))
        stage_o[DK] = dot(weight.astype(jnp.bfloat16), q2)
        stage_o[DV] = dot(attn_of(scores).astype(jnp.bfloat16), g2)

        @pl.when(side == 1)
        def _():
            totals[DQ, :, here] += stage_o[DQ]

        @pl.when(side == 0)
        def _():
            for kind in (DK, DV):
                totals[kind, :, here] += stage_o[kind]

    early = jnp.logical_not(led | plain)
    joins_k, joins_q = early & (side == 1), early & (side == 0)
    pl.when(early)(own_pair)
    every = [(j, r) for r in range(parts) for j in range(2)]

    def mover_give(i, j, r):
        kind = jnp.where(first_core, DQ, DK) + i
        return give(
            kind,
            0,
            stage_m.at[i, r, pl.ds(j * rp, rp)],
            r,
            ret_send_m.at[i, j, r],
            base_m + j,
        )

    def resident_give(i, j, r):
        kind = jnp.where(first_core, DK, DQ) + i
        return give(
            kind, 0, stage_r.at[i, j, part(r)], r, ret_send_r.at[i, j, r], base_r + j
        )

    far_j = 2 * core
    near_j = 2 * (1 - core)
    flat = 4 * rp

    @pl.when(is_main)
    def _():
        for j in range(2):
            for i in range(2):
                arrive(resident_c + i, base_r + far_j + j)
        for j in range(4):
            for i in range(2):
                block = inbox[resident_c + i, base_r + j]
                plain_r[i, j] = block.astype(jnp.bfloat16)
                stk_r[i, j] = stacked(block)

    def resident_major(both, first):
        blocks = slice(first, first + 2)
        left_c = plain_r[0, blocks].reshape(2 * rows, lane)
        left_d = plain_r[1, blocks].reshape(2 * rows, lane)
        grad_c = grad_d = None
        for r in range(parts):
            for h in range(2):
                a2, b2 = stk_m[0, r, h], stk_m[1, r, h]
                scores = rows_dot(left_c, a2)
                products = rows_dot(left_d, b2)
                term = dot(pgrad_of(scores, products).astype(jnp.bfloat16), a2)
                grad_c = term if grad_c is None else grad_c + term
                if both:
                    term = dot(attn_of(scores).astype(jnp.bfloat16), b2)
                    grad_d = term if grad_d is None else grad_d + term
        stage_r[0, blocks] = grad_c.reshape(2, rows, lane)
        if both:
            stage_r[1, blocks] = grad_d.reshape(2, rows, lane)

    def join_resident(kinds, block):
        for i, kind in enumerate(kinds):
            stage_r[i, near_j + block] += stage_o[kind]

    def far_gives(arrays):
        return [resident_give(i, far_j + j, q) for q in range(parts) for j in range(2) for i in arrays]

    def near_gives(arrays):
        return [resident_give(i, near_j + 1 - side, q) for q in range(parts) for i in arrays]

    for r in range(parts):

        @pl.when(is_main)
        def _(r=r):
            for j in range(4):
                for i in range(2):
                    arrive(mover_a + i, base_m + j, r)
            for j in range(4):
                for i in range(2):
                    block = inbox[mover_a + i, base_m + j, part(r)]
                    low, high = masked(block)
                    at = slice(j * rp, (j + 1) * rp)
                    plain_m[i, r, at] = block.astype(jnp.bfloat16)
                    stk_m[i, r, 0, at] = low
                    stk_m[i, r, 1, at] = high

        def mover_major(both, r):
            grad_a = grad_b = None
            for j in range(4):
                scores = rows_dot(plain_m[0, r], stk_r[0, j])
                products = rows_dot(plain_m[1, r], stk_r[1, j])
                term = dot(pgrad_of(scores, products).astype(jnp.bfloat16), stk_r[0, j])
                grad_a = term if grad_a is None else grad_a + term
                if both:
                    term = dot(attn_of(scores).astype(jnp.bfloat16), stk_r[1, j])
                    grad_b = term if grad_b is None else grad_b + term
            stage_m[0, r] = grad_a
            if both:
                stage_m[1, r] = grad_b

        if r == parts - 1:
            pl.when(is_main & first_core)(lambda: resident_major(True, 0))
            launch(is_main & first_core, far_gives((0, 1)))
            pl.when(is_main & first_core)(lambda: resident_major(True, 2))
            pl.when(is_main & joins_k)(lambda: join_resident((DK, DV), 0))
            launch(is_main & first_core, near_gives((0, 1)))
            for n in range(parts):
                pl.when(is_main & first_core)(lambda: mover_major(False, n))
                launch(is_main & first_core, [mover_give(0, j, n) for j in range(4)])
        pl.when(is_main & (core == 1))(lambda: mover_major(True, r))
        launch(is_main & (core == 1), [mover_give(i, j, r) for j in range(4) for i in range(2)])

    pl.when(is_main & (core == 1))(lambda: resident_major(False, 2))
    launch(is_main & (core == 1), far_gives((0,)))
    pl.when(is_main & (core == 1))(lambda: resident_major(False, 0))
    pl.when(is_main & joins_q)(lambda: join_resident((DQ,), 1))
    launch(is_main & (core == 1), near_gives((0,)))

    @pl.when(is_main & first_core)
    def _():
        totals[DK, :, here] += stage_r[0, near_j + side]
        totals[DV, :, here] += stage_r[1, near_j + side]

    @pl.when(is_main & (core == 1))
    def _():
        totals[DQ, :, here] += stage_r[0, near_j + side]

    @pl.when(outer)
    def _():
        from_line = jnp.where(line == 0, 1, 2)
        for j in range(2):
            for i in range(2):
                arrive(Q - needed + i, 2 * from_line + j)

    def pair_part(w, at_line, j):
        return inbox[w, 2 * at_line + j]

    @pl.when(outer)
    def _():
        k_blocks = [pair_part(K, s_line, j) for j in range(2)]
        v_blocks = [pair_part(V, s_line, j) for j in range(2)]
        k2 = jnp.concatenate([stacked(b) for b in k_blocks], axis=0)
        v2 = jnp.concatenate([stacked(b) for b in v_blocks], axis=0)
        for j in range(2):
            q = pair_part(Q, t_line, j).astype(jnp.bfloat16)
            g = pair_part(G, t_line, j).astype(jnp.bfloat16)
            weight = pgrad_of(rows_dot(q, k2), rows_dot(g, v2))
            stage_a[DQ, j] = dot(weight.astype(jnp.bfloat16), k2)
        q2 = jnp.concatenate([stacked(pair_part(Q, t_line, j)) for j in range(2)], axis=0)
        g2 = jnp.concatenate([stacked(pair_part(G, t_line, j)) for j in range(2)], axis=0)
        for j in range(2):
            scores = rows_dot(k_blocks[j].astype(jnp.bfloat16), q2)
            products = rows_dot(v_blocks[j].astype(jnp.bfloat16), g2)
            stage_a[DK, j] = dot(pgrad_of(scores, products).astype(jnp.bfloat16), q2)
            stage_a[DV, j] = dot(attn_of(scores).astype(jnp.bfloat16), g2)

    @pl.when(outer & joins_k)
    def _():
        for kind in (DK, DV):
            stage_a[kind, 0] += stage_o[kind]

    @pl.when(outer & joins_q)
    def _():
        stage_a[DQ, 1] += stage_o[DQ]

    def pair_give(kind, j, r, target):
        slot = jnp.where(target == other, 1, 0)
        return give(kind, slot, stage_a.at[kind, j, part(r)], r, ret_send_a.at[kind, j, r], target)

    def pair_gives(kinds, j, target):
        return [pair_give(kind, j, r, target) for r in range(parts) for kind in kinds]

    t_here, s_here = line == 3, line == 0
    launch(s_here, [c for j in range(2) for c in pair_gives((DQ,), j, 2 * t_line + j)])
    launch(s_here, pair_gives((DK, DV), 1 - side, other))
    launch(t_here, [c for j in range(2) for c in pair_gives((DK, DV), j, 2 * s_line + j)])
    launch(t_here, pair_gives((DQ,), 1 - side, other))

    @pl.when(t_here)
    def _():
        totals[DQ, :, here] += stage_a[DQ, side]

    @pl.when(s_here)
    def _():
        for kind in (DK, DV):
            totals[kind, :, here] += stage_a[kind, side]

    @pl.when(led)
    def _():
        for i in range(2):
            arrive(2 - lead + i, other)

    late = led | plain
    pl.when(late)(own_pair)

    def own_give(kind, r):
        return give(kind, 2, stage_o.at[kind, part(r)], r, ret_send_o.at[kind, r], other)

    launch(late & (side == 0), [own_give(DQ, r) for r in range(parts)])
    launch(late & (side == 1), [own_give(kind, r) for r in range(parts) for kind in (DK, DV)])

    def taken(kind, slot, p):
        away = side != p
        if slot == 2:
            wanted = side == (1 if kind == DQ else 0)
            other_needed = needed == (Q if kind == DQ else K)
            return away & wanted & (plain | jnp.logical_not(other_needed))
        if kind == DQ:
            if slot == 0:
                return (line > 0) & jnp.where(is_main & (core == 1), away, True)
            return (line == 3) & away
        if slot == 0:
            return (line < 3) & jnp.where(is_main & first_core, away, True)
        return (line == 0) & away

    def take(kind, slot, p, r):
        ref = ret.at[kind, slot, p, part(r)]
        remote(ref, ref, side_send.at[0], ret_recv.at[kind, slot, p, r], other).wait_recv()
        at = slice(r * rp, (r + 1) * rp)
        cols = slice(lane * p, lane * (p + 1))
        totals[kind, at, cols] += ret[kind, slot, p, at]

    def collect(r):
        for slot in (2, 1, 0):
            for kinds in ((DQ,), (DK, DV)):
                for p in range(pairs):

                    @pl.when(taken(kinds[0], slot, p))
                    def _():
                        for kind in kinds:
                            take(kind, slot, p, r)

    def to_head(source, target_ref, n, target):
        return pltpu.make_async_remote_copy(
            src_ref=source,
            dst_ref=target_ref,
            send_sem=reduce_send_sem.at[n],
            recv_sem=reduce_recv_sem.at[n],
            device_id={"head": target},
            device_id_type=MESH,
        )

    def to_core(r, n):
        return to_head(core_send_buf.at[r, n], core_recv_buf.at[r, n], 3 * r + n, core_mate)

    def to_out(r):
        return pltpu.make_async_copy(
            own_part.at[part(r)], own_out.at[part(r)], out_sem.at[r]
        )

    def to_far(r):
        return to_head(far_send_buf.at[r], far_out.at[part(r)], 3 * r + 2, far_mate)

    for r in range(parts):
        collect(r)
        at = slice(r * rp, (r + 1) * rp)
        if r == 0:
            for copy in weight_copies:
                copy.wait()
        final = [totals[i, at].astype(jnp.bfloat16) for i in range(3)]

        def project(target):
            cols = pl.ds(pl.multiple_of(target * out_width, out_width), out_width)
            return sum(dot(final[i], weights[i, :, cols]) for i in range(3))

        core_send_buf[r, 0] = project(2 * (1 - far) + (1 - core))
        to_core(r, 0).start()
        far_send_buf[r] = project(far_mate)
        core_send_buf[r, 1] = project(core_mate)
        to_core(r, 1).start()
        to_core(r, 0).wait_recv()
        far_send_buf[r] += core_recv_buf[r, 0]
        to_far(r).start()
        own_part[at] = project(head)

    for r in range(parts):
        at = slice(r * rp, (r + 1) * rp)
        to_core(r, 1).wait_recv()
        own_part[at] += core_recv_buf[r, 1]
        to_out(r).start()
    for r in range(parts):
        to_far(r).wait_recv()
        to_out(r).wait()

    for r in range(parts):
        to_core(r, 0).wait_send()
        to_core(r, 1).wait_send()
        to_far(r).wait_send()
    for cond, copies in pending:
        if cond is None:
            for copy in copies:
                copy.wait_send()
        else:

            @pl.when(cond)
            def _(copies=copies):
                for copy in copies:
                    copy.wait_send()


def routed_form(n_head, queries, keys, values, out_grad, w_query, w_key, w_value):
    rows, width = queries.shape
    model = w_query.shape[1]
    out_width = model // n_head
    pairs = width // (2 * HD)
    lane = 2 * HD
    blocks = 2 * LINES
    parts = 2
    rp = rows // parts
    f32, bf16 = jnp.float32, jnp.bfloat16
    dma = pltpu.SemaphoreType.DMA
    own_sum, far_sum = pl.pallas_call(
        functools.partial(routed_kernel, parts),
        out_shape=[jax.ShapeDtypeStruct((rows, out_width), f32)] * 2,
        in_specs=[pl.BlockSpec(memory_space=pl.ANY)] * 7,
        out_specs=[pl.BlockSpec(memory_space=pl.ANY)] * 2,
        scratch_shapes=[
            pltpu.VMEM((4, rows, width), bf16),
            pltpu.VMEM((4, pairs, rows, lane), f32),
            pltpu.VMEM((4, blocks, rows, lane), f32),
            pltpu.VMEM((2, 4, rows, lane), bf16),
            pltpu.VMEM((2, 4, 2 * rows, lane), bf16),
            pltpu.VMEM((2, parts, 4 * rp, lane), bf16),
            pltpu.VMEM((2, parts, 2, 4 * rp, lane), bf16),
            pltpu.VMEM((2, parts, 4 * rp, lane), f32),
            pltpu.VMEM((2, 4, rows, lane), f32),
            pltpu.VMEM((3, 2, rows, lane), f32),
            pltpu.VMEM((3, rows, lane), f32),
            pltpu.VMEM((3, 3, pairs, rows, lane), f32),
            pltpu.VMEM((3, width, model), bf16),
            pltpu.VMEM((3, rows, width), f32),
            pltpu.VMEM((rows, out_width), f32),
            pltpu.VMEM((parts, 2, rp, out_width), f32),
            pltpu.VMEM((parts, 2, rp, out_width), f32),
            pltpu.VMEM((parts, rp, out_width), f32),
            dma((4,)),
            dma((3,)),
            dma((parts,)),
            dma((2, pairs, parts)),
            dma((2, pairs)),
            dma((2, pairs)),
            dma((6,)),
            dma((4, blocks, parts)),
            dma((3, 3, pairs, parts)),
            dma((2, 4, parts)),
            dma((2, 4, parts)),
            dma((3, 2, parts)),
            dma((3, parts)),
            dma((3 * parts,)),
            dma((3 * parts,)),
        ],
        compiler_params=pltpu.CompilerParams(collective_id=0, has_side_effects=True),
    )(keys, values, queries, out_grad, w_query, w_key, w_value)
    return (own_sum + far_sum).astype(bf16)


def solution(mesh):
    placed = (
        P("seq", "head"),
        P("seq", "head"),
        P("seq", "head"),
        P("seq", "head"),
        P("head", None),
        P("head", None),
        P("head", None),
    )
    n_seq, n_head = mesh.shape["seq"], mesh.shape["head"]

    def per_device(queries, *rest):
        if n_seq == 2 * LINES and n_head == 4 and queries.shape[1] == 4 * HD:
            return routed_form(n_head, queries, *rest)
        return on_device(queries, *rest)

    return jax.shard_map(
        per_device, mesh=mesh, in_specs=placed, out_specs=P("seq", "head"), check_vma=False
    )
```
